512 devices in a mesh: gx: 32 (over z, core), gy: 16 (over x, y).
Axes of the slice: x: 4, y: 4, z: 16, core: 2. Of those that a mesh axis runs over, the one named last changes fastest.
Arguments:
- probes: bfloat16 [8, 4194304], P(None, ('gx', 'gy')), may hold values from -6 to 6
- cells: int32 [3, 4194304], P(None, ('gx', 'gy')), may hold values from 0 to 1023, as said below
- fractions: float32 [3, 4194304], P(None, ('gx', 'gy')), may hold values from 0 to 1
- counts: int32 [32, 16], P('gx', 'gy'), may hold values from 0 to 64, as said below
- kx: bfloat16 [1024, 1024], P('gx'), may hold values from 0 to 1
- ky: bfloat16 [1024, 1024], P('gy'), may hold values from 0 to 1
- kt: float32 [4, 4], replicated, may hold values from 0.25 to 1
Outputs:
- applied: bfloat16 [8, 4194304], P(None, ('gx', 'gy'))
The draws below stay inside these ranges and needn't reach their ends.
Inputs may be any that keep to these rules, and one draw needn't show every extreme that they name: cells[0] lies in the x rows 32 * i to 32 * i + 31 and cells[1] in the y columns 64 * j to 64 * j + 63, where the slot lies on the device at index i of gx and j of gy; cells[2] is below 3. `counts`: slots of blocks at or past a device's count hold no observation; some device has 64 live blocks.
All inputs are finite; a program needn't handle non-finite values.
Results may differ from the reference program's by a relative error of at most 0.002.
The reference program's roundings to bfloat16 on the way count: a program that leaves them out, or rounds other values in their place, can miss the bound.
Values may be sent and summed in bfloat16 or wider, within the bound.
No kernel may reach another device: no remote copies, remote signals or barrier semaphores. Data moves between devices by JAX's collectives and lax.ppermute only.
A program may use at most 64 MiB of HBM per device.

```python
import jax
import jax.numpy as jnp
from jax import lax

NX = 1024
NY = 1024
DAYS = 4
PROBES = 8
BLOCK = 128
BLK_DEV = 64
PTS_DEV = 8192
NPTS = 4194304
TILES_X = 32
TILES_Y = 16
CX = 32
CY = 64
ELL_X = 512
ELL_Y = 512


def draw_cells(key, part):
    slots = jnp.arange(NPTS, dtype=jnp.int32)
    device = slots // PTS_DEV
    tile_x = device // TILES_Y
    tile_y = device % TILES_Y
    row_cell = tile_x * CX + jax.random.randint(jax.random.fold_in(key, 1), (NPTS,), 0, CX)
    col_cell = tile_y * CY + jax.random.randint(jax.random.fold_in(key, 2), (NPTS,), 0, CY)
    day_cell = jax.random.randint(jax.random.fold_in(key, 3), (NPTS,), 0, DAYS - 1)
    return jnp.stack([row_cell, col_cell, day_cell]).astype(jnp.int32)


def draw_counts(key, part):
    tiles = TILES_X * TILES_Y
    drawn_root = jax.random.randint(jax.random.fold_in(key, 11), (tiles,), 0, BLK_DEV + 1)
    loads = drawn_root * drawn_root // BLK_DEV
    fullest = jax.random.randint(jax.random.fold_in(key, 12), (), 0, tiles)
    loads = jnp.where(jnp.arange(tiles, dtype=jnp.int32) == fullest, BLK_DEV, loads)
    return loads.reshape(TILES_X, TILES_Y).astype(jnp.int32)


def kernel_factor(key, order, reach_cells, roughness):
    position = jnp.arange(order, dtype=jnp.float32)
    distance = jnp.abs(position[:, None] - position[None, :])
    return jnp.exp(-distance / reach_cells) * roughness / jnp.sqrt(jnp.float32(reach_cells))


def draw_kx(key, part):
    roughness = jax.random.uniform(jax.random.fold_in(key, 21), (NX, NX), jnp.float32, 0.5, 1.5)
    return kernel_factor(key, NX, ELL_X, roughness).astype(jnp.bfloat16)


def draw_ky(key, part):
    roughness = jax.random.uniform(jax.random.fold_in(key, 31), (NY, NY), jnp.float32, 0.5, 1.5)
    return kernel_factor(key, NY, ELL_Y, roughness).astype(jnp.bfloat16)


def levels(key, dims, shards, low, top_value):
    def one(dim, blocks):
        heights = jax.random.uniform(jax.random.fold_in(jax.random.fold_in(key, 6), dim), (blocks,), jnp.float32, low / len(shards), top_value / len(shards))
        return jnp.repeat(jnp.exp(heights), dims[dim] // blocks).reshape((-1,) + (1,) * (len(dims) - dim - 1))

    level = one(*shards[0])
    for cut in shards[1:]:
        level = level * one(*cut)
    return level


def scatter_about(own_key, shape, scale, bound, pieces=(), kind=jnp.bfloat16):
    array = jax.random.normal(own_key, shape, jnp.float32) * scale
    if len(pieces) > 0:
        array = levels(own_key, shape, pieces, -0.22, 0.18) * array
    return jnp.clip(array, min=-bound, max=bound).astype(kind)


def setup_inputs(seed: int = 0) -> dict:
    key_list = jax.random.split(jax.random.key(seed), 8)
    probes = scatter_about(key_list[0], (PROBES, NPTS), 1.0, 6.0, ((1, 512),))
    cells = draw_cells(jax.random.fold_in(key_list[7], 71), 0)
    fractions = jnp.clip(1.0 * jax.random.uniform(key_list[2], (3, NPTS), jnp.float32) ** levels(key_list[2], (3, NPTS), ((1, 512),), -0.2, 0.2), 0.0, 1.0)
    counts = draw_counts(jax.random.fold_in(key_list[7], 71), 0)
    kx = draw_kx(jax.random.fold_in(key_list[7], 71), 0)
    ky = draw_ky(jax.random.fold_in(key_list[7], 71), 0)
    kt = jnp.clip(jax.random.uniform(key_list[6], (DAYS, DAYS), jnp.float32, 0.25, 1.0), 0.25, 1.0)
    return {"probes": probes, "cells": cells, "fractions": fractions, "counts": counts, "kx": kx, "ky": ky, "kt": kt}


def keys_weights(fraction):
    first = ((-0.5 * fraction + 1.0) * fraction - 0.5) * fraction
    second = (1.5 * fraction - 2.5) * fraction * fraction + 1.0
    third = ((-1.5 * fraction + 2.0) * fraction + 0.5) * fraction
    fourth = (0.5 * fraction - 0.5) * fraction * fraction
    return (first, second, third, fourth)


def reference(probes, cells, fractions, counts, kx, ky, kt):
    points = probes.shape[1]
    slots = jnp.arange(points, dtype=jnp.int32)
    device = slots // PTS_DEV
    live_mask = ((slots % PTS_DEV) // BLOCK < counts.reshape(-1)[device]).astype(jnp.float32)
    row_cell = cells[0]
    col_cell = cells[1]
    day_cell = cells[2]
    weights_x = keys_weights(fractions[0])
    weights_y = [lax.optimization_barrier(w_part.astype(jnp.bfloat16)).astype(jnp.float32) for w_part in keys_weights(fractions[1])]
    weights_t = (1.0 - fractions[2], fractions[2])
    values = probes.astype(jnp.float32) * live_mask[None, :]
    channel = jnp.arange(PROBES, dtype=jnp.int32)
    grid_sum = jnp.zeros((DAYS, PROBES, NX + 3, NY + 3), jnp.float32)
    for step_x in range(4):
        for step_t in range(2):
            timed_values = weights_t[step_t][None, :] * values
            weighted = lax.optimization_barrier((timed_values * weights_x[step_x][None, :]).astype(jnp.bfloat16)).astype(jnp.float32)
            for step_y in range(4):
                grid_sum = grid_sum.at[(day_cell + step_t)[None, :], channel[:, None], (row_cell + step_x)[None, :], (col_cell + step_y)[None, :]].add(weighted * weights_y[step_y][None, :])
    grid_sum = grid_sum[:, :, 1:NX + 1, 1:NY + 1].astype(jnp.bfloat16)
    mixed_x = jnp.einsum("xz,tqzy->tqxy", kx.astype(jnp.float32), grid_sum.astype(jnp.float32), precision=lax.Precision.HIGHEST).astype(jnp.bfloat16)
    crossed = jnp.einsum("yz,tqxz->tqxy", ky.astype(jnp.float32), mixed_x.astype(jnp.float32), precision=lax.Precision.HIGHEST)
    smooth = jnp.einsum("st,tqxy->sqxy", kt, crossed, precision=lax.Precision.HIGHEST).astype(jnp.bfloat16)
    padded = jnp.pad(smooth.astype(jnp.float32), ((0, 0), (0, 0), (1, 2), (1, 2)))
    result = jnp.zeros((PROBES, points), jnp.float32)
    for step_x in range(4):
        inner_sum = jnp.zeros((PROBES, points), jnp.float32)
        for step_t in range(2):
            line_sum = jnp.zeros((PROBES, points), jnp.float32)
            for step_y in range(4):
                picked = padded[day_cell + step_t, :, row_cell + step_x, col_cell + step_y]
                line_sum = line_sum + weights_y[step_y][None, :] * picked.T
            inner_sum = inner_sum + weights_t[step_t][None, :] * line_sum
        result = result + weights_x[step_x][None, :] * inner_sum
    return (result * live_mask[None, :]).astype(jnp.bfloat16)
```

```python
import jax
import jax.numpy as jnp
from jax import lax
from jax.experimental import pallas as pl
from jax.experimental.pallas import tpu as pltpu
from jax.sharding import Mesh
from jax.sharding import PartitionSpec as P

DAYS = 4
PROBES = 8
BLOCK = 128
ROWS = 32
COLS = 64
XP = 40
YP = 80
CHUNK = 512
AXES = ("zh", "zl", "c", "x", "y")
GX = ("zh", "zl", "c")
NEAR = ("zl", "c")
GY = ("x", "y")
HIGH = lax.Precision.HIGHEST


def keys_weights(fraction):
    first = ((-0.5 * fraction + 1.0) * fraction - 0.5) * fraction
    second = (1.5 * fraction - 2.5) * fraction * fraction + 1.0
    third = ((-1.5 * fraction + 2.0) * fraction + 0.5) * fraction
    fourth = (0.5 * fraction - 0.5) * fraction * fraction
    return (first, second, third, fourth)


def spread(cell, weights, extent):
    row = lax.broadcasted_iota(jnp.int32, (extent, cell.shape[1]), 0) - cell
    result = jnp.where(row == 3, weights[3], 0.0)
    for k in (2, 1, 0):
        result = jnp.where(row == k, weights[k], result)
    return result


def point_factors(cells_ref, fractions_ref, where):
    x_part = spread(
        cells_ref[0:1, where] % ROWS, keys_weights(fractions_ref[0:1, where]), XP
    )
    y_part = spread(
        cells_ref[1:2, where] % COLS, keys_weights(fractions_ref[1:2, where]), YP
    )
    day = cells_ref[2:3, where]
    y_days = [jnp.where(day == d, y_part, 0.0) for d in range(DAYS - 1)]
    y_days.append(jnp.zeros((256 - 3 * YP, y_part.shape[1]), jnp.float32))
    y_days = jnp.concatenate(y_days, axis=0).astype(jnp.bfloat16)
    late = fractions_ref[2:3, where]
    return x_part, y_days, 1.0 - late, late


def live_lanes(count_ref, start, size):
    slot = start + lax.broadcasted_iota(jnp.int32, (1, size), 1)
    return slot // BLOCK < count_ref[0, 0]


def scatter_kernel(count_ref, probes_ref, cells_ref, fractions_ref, core_ref, rim_ref, acc_ref):
    points = probes_ref.shape[1]
    acc_ref[...] = jnp.zeros_like(acc_ref)

    def step(number, carry):
        start = pl.multiple_of(number * CHUNK, CHUNK)
        where = pl.ds(start, CHUNK)
        x_part, y_days, early, late = point_factors(cells_ref, fractions_ref, where)
        values = jnp.where(
            live_lanes(count_ref, start, CHUNK), probes_ref[:, where].astype(jnp.float32), 0.0
        )
        parts = []
        for weight in (early, late):
            timed = weight * values
            for q in range(PROBES):
                parts.append(timed[q : q + 1] * x_part)
        weighted = jnp.concatenate(parts, axis=0).astype(jnp.bfloat16)
        acc_ref[...] += lax.dot_general(
            weighted, y_days, (((1,), (1,)), ((), ())), preferred_element_type=jnp.float32
        )
        return carry

    lax.fori_loop(0, points // CHUNK, step, 0)
    rows = PROBES * XP
    blank = jnp.zeros((rows, 128), jnp.float32)
    first = jnp.concatenate([acc_ref[0:rows, :], blank], axis=1)
    second = jnp.concatenate([acc_ref[rows : 2 * rows, :], blank], axis=1)
    total = first + pltpu.roll(second, YP, 1)
    lane = lax.broadcasted_iota(jnp.int32, (rows, 384), 1)
    core = pltpu.roll(total, 383, 1)
    for t in range(1, DAYS):
        core = jnp.where(lane // COLS == t, pltpu.roll(total, 384 - (16 * t + 1), 1), core)
    core_ref[...] = core[:, 0:256]
    out_row = lax.broadcasted_iota(jnp.int32, (16, 384), 0)
    in_lane = lax.broadcasted_iota(jnp.int32, (16, 384), 1)
    low = (out_row < DAYS) & (in_lane == YP * out_row)
    high_row = out_row - 8
    high = (high_row >= 0) & (in_lane == YP * (high_row // 2) + (COLS + 1) + high_row % 2)
    pick = jnp.where(low | high, 1.0, 0.0)
    rim_ref[...] = lax.dot_general(
        pick, total, (((1,), (1,)), ((), ())), precision=HIGH, preferred_element_type=jnp.float32
    )


def scatter(counts, probes, cells, fractions):
    rows = PROBES * XP
    return pl.pallas_call(
        scatter_kernel,
        out_shape=(
            jax.ShapeDtypeStruct((rows, 256), jnp.float32),
            jax.ShapeDtypeStruct((16, rows), jnp.float32),
        ),
        in_specs=[
            pl.BlockSpec(memory_space=pltpu.SMEM),
            pl.BlockSpec(memory_space=pltpu.VMEM),
            pl.BlockSpec(memory_space=pltpu.VMEM),
            pl.BlockSpec(memory_space=pltpu.VMEM),
        ],
        scratch_shapes=[pltpu.VMEM((2 * rows, 256), jnp.float32)],
        name="scatter",
    )(counts, probes, cells, fractions)


def add_cols_kernel(core_ref, low_ref, high_ref, out_ref, first_ref, last_ref):
    row = lax.broadcasted_iota(jnp.int32, (16, 256), 0)
    lane = lax.broadcasted_iota(jnp.int32, (16, 256), 1)
    high_row = row - 8
    put = (row < DAYS) & (lane == COLS * row + (COLS - 1))
    put = put | ((high_row >= 0) & (lane == COLS * (high_row // 2) + high_row % 2))
    received = jnp.concatenate([low_ref[...], high_ref[...]], axis=0)
    out_ref[...] = core_ref[...] + lax.dot_general(
        received,
        jnp.where(put, 1.0, 0.0),
        (((0,), (0,)), ((), ())),
        precision=HIGH,
        preferred_element_type=jnp.float32,
    )
    first, last = [], []
    for q in range(PROBES):
        first.append(out_ref[q * XP : q * XP + 1, :])
        last.append(out_ref[q * XP + ROWS + 1 : q * XP + ROWS + 3, :])
    first_ref[...] = jnp.concatenate(first, axis=0)
    last_ref[...] = jnp.concatenate(last, axis=0)


def add_cols(core, low, high):
    return pl.pallas_call(
        add_cols_kernel,
        out_shape=(
            jax.ShapeDtypeStruct(core.shape, jnp.float32),
            jax.ShapeDtypeStruct((PROBES, 256), jnp.float32),
            jax.ShapeDtypeStruct((2 * PROBES, 256), jnp.float32),
        ),
        name="add_cols",
    )(core, low, high)


def add_rows_kernel(core_ref, first_ref, last_ref, out_ref):
    row = lax.broadcasted_iota(jnp.int32, (ROWS, 256), 0)
    for q in range(PROBES):
        tile = core_ref[q * XP + 1 : q * XP + 1 + ROWS, :]
        extra = jnp.where(row == ROWS - 1, first_ref[q : q + 1, :], 0.0)
        extra = jnp.where(row == 0, last_ref[2 * q : 2 * q + 1, :], extra)
        extra = jnp.where(row == 1, last_ref[2 * q + 1 : 2 * q + 2, :], extra)
        tile = (tile + extra).astype(jnp.bfloat16)
        for copy in range(4):
            out_ref[copy * PROBES + q] = tile


def add_rows(core, first, last):
    return pl.pallas_call(
        add_rows_kernel,
        out_shape=jax.ShapeDtypeStruct((4 * PROBES, ROWS, 256), jnp.bfloat16),
        name="add_rows",
    )(core, first, last)


def mix_x_kernel(place_ref, grid_ref, k0_ref, k1_ref, k2_ref, k3_ref, out_ref, rows_ref):
    zl, core = place_ref[0], place_ref[1]
    kernel = jnp.concatenate([k0_ref[...], k1_ref[...], k2_ref[...], k3_ref[...]], axis=0)
    mixed = jnp.dot(kernel, grid_ref[...], preferred_element_type=jnp.float32)
    rows_ref[0:8, :] = jnp.zeros((8, 256), jnp.float32)
    rows_ref[264:272, :] = jnp.zeros((8, 256), jnp.float32)
    for shift in range(4):
        source = (zl + 4 - shift) % 4
        for half in range(2):
            from_core = core if half == 0 else 1 - core
            base = (2 * shift + half) * XP
            target = pl.multiple_of(8 + ROWS * (2 * source + from_core), 8)
            rows_ref[pl.ds(target, ROWS), :] = mixed[base : base + ROWS]

            @pl.when((source == 3) & (from_core == 1))
            def _():
                rows_ref[7:8, :] = mixed[base + ROWS : base + ROWS + 1]

            @pl.when((source == 0) & (from_core == 0))
            def _():
                rows_ref[264:266, :] = mixed[base + ROWS + 1 : base + ROWS + 3]

    for tile in range(8):
        out_ref[tile] = rows_ref[7 + ROWS * tile : 7 + ROWS * tile + XP, :].astype(jnp.bfloat16)


def mix_x(place, grid, pieces):
    return pl.pallas_call(
        mix_x_kernel,
        out_shape=jax.ShapeDtypeStruct((8, XP, 256), jnp.bfloat16),
        in_specs=[pl.BlockSpec(memory_space=pltpu.SMEM)]
        + [pl.BlockSpec(memory_space=pltpu.VMEM)] * 5,
        scratch_shapes=[pltpu.VMEM((272, 256), jnp.float32)],
        name="mix_x",
    )(place, grid, *pieces)


def gather_kernel(
    count_ref, kt_ref, mixed_ref, ky_ref, cells_ref, fractions_ref, out_ref, window_ref
):
    points = out_ref.shape[1]
    rows = PROBES * XP
    lane = lax.broadcasted_iota(jnp.int32, (YP, 128), 1)
    gap = jnp.zeros((128 - YP, 256), jnp.float32)
    crossed = [jnp.zeros((rows, 256), jnp.float32) for _ in range(2)]
    for pair in range(8):
        here = ky_ref[:, 128 * pair : 128 * pair + 128].astype(jnp.float32)
        turned = pltpu.roll(here, COLS, 1)
        low, high = lane < COLS, lane >= COLS
        even = jnp.concatenate([jnp.where(low, here, 0.0), jnp.where(low, turned, 0.0)], axis=1)
        odd = jnp.concatenate([jnp.where(high, turned, 0.0), jnp.where(high, here, 0.0)], axis=1)
        kernel = jnp.concatenate([even, gap, odd, gap], axis=0).astype(jnp.bfloat16)
        for half in range(2):
            side = slice(128 * half, 128 * half + 128)
            left = jnp.concatenate(
                [mixed_ref[2 * pair, :, side], mixed_ref[2 * pair + 1, :, side]], axis=1
            )
            crossed[half] += lax.dot_general(
                left, kernel, (((1,), (1,)), ((), ())), preferred_element_type=jnp.float32
            )
    by_day = [crossed[t // 2][:, 128 * (t % 2) : 128 * (t % 2) + 128] for t in range(DAYS)]
    blank = jnp.zeros((rows, 128), jnp.float32)
    smooth = []
    for s in range(DAYS):
        total = kt_ref[s, 0] * by_day[0]
        for t in range(1, DAYS):
            total = total + kt_ref[s, t] * by_day[t]
        total = total.astype(jnp.bfloat16).astype(jnp.float32)
        smooth.append(jnp.concatenate([total, blank], axis=1))
    for late in range(2):
        window = smooth[late] + pltpu.roll(smooth[late + 1], YP, 1)
        window = window + pltpu.roll(smooth[late + 2], 2 * YP, 1)
        window_ref[late * rows : (late + 1) * rows, :] = window.astype(jnp.bfloat16)

    def step(number, carry):
        start = pl.multiple_of(number * CHUNK, CHUNK)
        where = pl.ds(start, CHUNK)
        x_part, y_days, early, late = point_factors(cells_ref, fractions_ref, where)
        hidden = jnp.dot(window_ref[...], y_days, preferred_element_type=jnp.float32)
        timed = early * hidden[0:rows] + late * hidden[rows : 2 * rows]
        sums = []
        for q in range(PROBES):
            sums.append(
                jnp.sum(timed[q * XP : (q + 1) * XP] * x_part, axis=0, keepdims=True)
            )
        result = jnp.concatenate(sums, axis=0)
        result = jnp.where(live_lanes(count_ref, start, CHUNK), result, 0.0)
        out_ref[:, where] = result.astype(jnp.bfloat16)
        return carry

    lax.fori_loop(0, points // CHUNK, step, 0)


def gather(counts, kt, mixed, ky, cells, fractions):
    rows = PROBES * XP
    return pl.pallas_call(
        gather_kernel,
        out_shape=jax.ShapeDtypeStruct((PROBES, cells.shape[1]), jnp.bfloat16),
        in_specs=[pl.BlockSpec(memory_space=pltpu.SMEM)] * 2
        + [pl.BlockSpec(memory_space=pltpu.VMEM)] * 4,
        scratch_shapes=[pltpu.VMEM((2 * rows, 256), jnp.bfloat16)],
        name="gather",
    )(counts, kt, mixed, ky, cells, fractions)


def up(count):
    return [(i, i + 1) for i in range(count - 1)]


def down(count):
    return [(i + 1, i) for i in range(count - 1)]


def body(probes, cells, fractions, counts, kx, ky, kt):
    before = lax.ppermute(kx[ROWS - 1 : ROWS], "zh", up(4))
    after = lax.ppermute(kx[0:2], "zh", down(4))
    own = jnp.concatenate([kx, before, after, jnp.zeros((XP - ROWS - 3, 1024), kx.dtype)], axis=0)
    other = lax.ppermute(own, "c", [(0, 1), (1, 0)])
    pair = jnp.concatenate([own, other], axis=0)
    pieces = [pair]
    for shift in range(1, 4):
        pieces.append(lax.ppermute(pair, "zl", [(i, (i + shift) % 4) for i in range(4)]))
    left = lax.ppermute(ky[COLS - 1 : COLS], GY, up(16))
    right = lax.ppermute(ky[0:2], GY, down(16))
    ky_wide = jnp.concatenate(
        [left, ky, right, jnp.zeros((YP - COLS - 3, 1024), ky.dtype)], axis=0
    )

    core, rim = scatter(counts, probes, cells, fractions)
    low = lax.ppermute(rim[0:8], GY, down(16))
    high = lax.ppermute(rim[8:16], GY, up(16))
    core, first, last = add_cols(core, low, high)
    first = lax.ppermute(first, GX, down(32))
    last = lax.ppermute(last, GX, up(32))
    grid = add_rows(core, first, last)
    grid = lax.all_to_all(grid, GX, 0, 0, tiled=True)
    place = jnp.stack([lax.axis_index("zl"), lax.axis_index("c")]).astype(jnp.int32)
    mixed = mix_x(place, grid.reshape(32 * ROWS, 256), pieces)
    mixed = lax.all_to_all(mixed, NEAR, 0, 0, tiled=True)
    mixed = jnp.broadcast_to(mixed.reshape(1, PROBES * XP, 256), (16, PROBES * XP, 256))
    mixed = lax.all_to_all(mixed, GY, 0, 0, tiled=True)
    return gather(counts, kt, mixed, ky_wide, cells, fractions)


def solution(mesh):
    fine = Mesh(mesh.devices.reshape(4, 4, 2, 4, 4), AXES)
    return jax.shard_map(
        body,
        mesh=fine,
        in_specs=(
            P(None, AXES),
            P(None, AXES),
            P(None, AXES),
            P(GX, GY),
            P(GX, None),
            P(GY, None),
            P(),
        ),
        out_specs=P(None, AXES),
        check_vma=False,
    )
```

```python
import jax
import jax.numpy as jnp
from jax import lax
from jax.experimental import pallas as pl
from jax.experimental.pallas import tpu as pltpu
from jax.sharding import Mesh
from jax.sharding import PartitionSpec as P

DAYS = 4
PROBES = 8
BLOCK = 128
ROWS = 32
COLS = 64
XP = 40
YP = 80
CHUNK = 512
AXES = ("zh", "zl", "c", "x", "y")
GX = ("zh", "zl", "c")
NEAR = ("zl", "c")
GY = ("x", "y")
HIGH = lax.Precision.HIGHEST


def keys_weights(fraction):
    first = ((-0.5 * fraction + 1.0) * fraction - 0.5) * fraction
    second = (1.5 * fraction - 2.5) * fraction * fraction + 1.0
    third = ((-1.5 * fraction + 2.0) * fraction + 0.5) * fraction
    fourth = (0.5 * fraction - 0.5) * fraction * fraction
    return (first, second, third, fourth)


def spread(cell, weights, extent):
    row = lax.broadcasted_iota(jnp.int32, (extent, cell.shape[1]), 0) - cell
    result = jnp.where(row == 3, weights[3], 0.0)
    for k in (2, 1, 0):
        result = jnp.where(row == k, weights[k], result)
    return result


def point_factors(cells_ref, fractions_ref, where):
    x_part = spread(
        cells_ref[0:1, where] % ROWS, keys_weights(fractions_ref[0:1, where]), XP
    )
    y_part = spread(
        cells_ref[1:2, where] % COLS, keys_weights(fractions_ref[1:2, where]), YP
    )
    day = cells_ref[2:3, where]
    y_days = [jnp.where(day == d, y_part, 0.0) for d in range(DAYS - 1)]
    y_days.append(jnp.zeros((256 - 3 * YP, y_part.shape[1]), jnp.float32))
    y_days = jnp.concatenate(y_days, axis=0).astype(jnp.bfloat16)
    late = fractions_ref[2:3, where]
    return x_part, y_days, 1.0 - late, late


def live_lanes(count_ref, start, size):
    slot = start + lax.broadcasted_iota(jnp.int32, (1, size), 1)
    return slot // BLOCK < count_ref[0, 0]


def scatter_kernel(
    count_ref, probes_ref, cells_ref, fractions_ref, core_ref, low_ref, high_ref, acc_ref
):
    points = probes_ref.shape[1]
    acc_ref[...] = jnp.zeros_like(acc_ref)

    def step(number, carry):
        start = pl.multiple_of(number * CHUNK, CHUNK)
        where = pl.ds(start, CHUNK)
        x_part, y_days, early, late = point_factors(cells_ref, fractions_ref, where)
        values = jnp.where(
            live_lanes(count_ref, start, CHUNK), probes_ref[:, where].astype(jnp.float32), 0.0
        )
        parts = []
        for weight in (early, late):
            timed = weight * values
            for q in range(PROBES):
                parts.append(timed[q : q + 1] * x_part)
        weighted = jnp.concatenate(parts, axis=0).astype(jnp.bfloat16)
        acc_ref[...] += lax.dot_general(
            weighted, y_days, (((1,), (1,)), ((), ())), preferred_element_type=jnp.float32
        )
        return carry

    lax.fori_loop(0, points // CHUNK, step, 0)
    rows = PROBES * XP
    blank = jnp.zeros((rows, 128), jnp.float32)
    first = jnp.concatenate([acc_ref[0:rows, :], blank], axis=1)
    second = jnp.concatenate([acc_ref[rows : 2 * rows, :], blank], axis=1)
    total = first + pltpu.roll(second, YP, 1)
    lane = lax.broadcasted_iota(jnp.int32, (rows, 384), 1)
    core = pltpu.roll(total, 383, 1)
    for t in range(1, DAYS):
        core = jnp.where(lane // COLS == t, pltpu.roll(total, 384 - (16 * t + 1), 1), core)
    core_ref[...] = core[:, 0:256]
    out_row = lax.broadcasted_iota(jnp.int32, (16, 384), 0)
    in_lane = lax.broadcasted_iota(jnp.int32, (16, 384), 1)
    low = (out_row < DAYS) & (in_lane == YP * out_row)
    high_row = out_row - 8
    high = (high_row >= 0) & (in_lane == YP * (high_row // 2) + (COLS + 1) + high_row % 2)
    pick = jnp.where(low | high, 1.0, 0.0)
    rims = lax.dot_general(
        pick, total, (((1,), (1,)), ((), ())), precision=HIGH, preferred_element_type=jnp.float32
    )
    low_ref[...] = rims[0:8]
    high_ref[...] = rims[8:16]


def scatter(counts, probes, cells, fractions):
    rows = PROBES * XP
    return pl.pallas_call(
        scatter_kernel,
        out_shape=(
            jax.ShapeDtypeStruct((rows, 256), jnp.float32),
            jax.ShapeDtypeStruct((8, rows), jnp.float32),
            jax.ShapeDtypeStruct((8, rows), jnp.float32),
        ),
        in_specs=[
            pl.BlockSpec(memory_space=pltpu.SMEM),
            pl.BlockSpec(memory_space=pltpu.VMEM),
            pl.BlockSpec(memory_space=pltpu.VMEM),
            pl.BlockSpec(memory_space=pltpu.VMEM),
        ],
        scratch_shapes=[pltpu.VMEM((2 * rows, 256), jnp.float32)],
        name="scatter",
    )(counts, probes, cells, fractions)


def add_cols_kernel(core_ref, low_ref, high_ref, out_ref, first_ref, last_ref):
    row = lax.broadcasted_iota(jnp.int32, (16, 256), 0)
    lane = lax.broadcasted_iota(jnp.int32, (16, 256), 1)
    high_row = row - 8
    put = (row < DAYS) & (lane == COLS * row + (COLS - 1))
    put = put | ((high_row >= 0) & (lane == COLS * (high_row // 2) + high_row % 2))
    received = jnp.concatenate([low_ref[...], high_ref[...]], axis=0)
    out_ref[...] = core_ref[...] + lax.dot_general(
        received,
        jnp.where(put, 1.0, 0.0),
        (((0,), (0,)), ((), ())),
        precision=HIGH,
        preferred_element_type=jnp.float32,
    )
    first, last = [], []
    for q in range(PROBES):
        first.append(out_ref[q * XP : q * XP + 1, :])
        last.append(out_ref[q * XP + ROWS + 1 : q * XP + ROWS + 3, :])
    first_ref[...] = jnp.concatenate(first, axis=0)
    last_ref[...] = jnp.concatenate(last, axis=0)


def add_cols(core, low, high):
    return pl.pallas_call(
        add_cols_kernel,
        out_shape=(
            jax.ShapeDtypeStruct(core.shape, jnp.float32),
            jax.ShapeDtypeStruct((PROBES, 256), jnp.float32),
            jax.ShapeDtypeStruct((2 * PROBES, 256), jnp.float32),
        ),
        name="add_cols",
    )(core, low, high)


def add_rows_kernel(core_ref, first_ref, last_ref, out_ref):
    row = lax.broadcasted_iota(jnp.int32, (ROWS, 256), 0)
    for q in range(PROBES):
        tile = core_ref[q * XP + 1 : q * XP + 1 + ROWS, :]
        extra = jnp.where(row == ROWS - 1, first_ref[q : q + 1, :], 0.0)
        extra = jnp.where(row == 0, last_ref[2 * q : 2 * q + 1, :], extra)
        extra = jnp.where(row == 1, last_ref[2 * q + 1 : 2 * q + 2, :], extra)
        tile = (tile + extra).astype(jnp.bfloat16)
        for copy in range(4):
            out_ref[copy * PROBES + q] = tile


def add_rows(core, first, last):
    return pl.pallas_call(
        add_rows_kernel,
        out_shape=jax.ShapeDtypeStruct((4 * PROBES, ROWS, 256), jnp.bfloat16),
        name="add_rows",
    )(core, first, last)


def mix_x_kernel(place_ref, grid_ref, k0_ref, k1_ref, k2_ref, k3_ref, out_ref):
    zl, core = place_ref[0], place_ref[1]
    kernel = jnp.concatenate([k0_ref[...], k1_ref[...], k2_ref[...], k3_ref[...]], axis=0)
    mixed = jnp.dot(kernel, grid_ref[...], preferred_element_type=jnp.float32)
    for shift in range(4):
        tile = 2 * ((zl + 4 - shift) % 4)
        for half in range(2):
            base = (2 * shift + half) * XP
            part = mixed[base : base + XP].astype(jnp.bfloat16)
            out_ref[tile + (core if half == 0 else 1 - core)] = part


def mix_x(place, grid, pieces):
    return pl.pallas_call(
        mix_x_kernel,
        out_shape=jax.ShapeDtypeStruct((8, XP, 256), jnp.bfloat16),
        in_specs=[pl.BlockSpec(memory_space=pltpu.SMEM)]
        + [pl.BlockSpec(memory_space=pltpu.VMEM)] * 5,
        name="mix_x",
    )(place, grid, *pieces)


def mix_y_kernel(place_ref, kt_ref, mixed_ref, k0_ref, k1_ref, k2_ref, k3_ref, out_ref):
    rows = 2 * XP
    low = lax.broadcasted_iota(jnp.int32, (rows, 128), 1) < COLS
    left = [[] for _ in range(DAYS)]
    for pair in range(8):
        even = mixed_ref[2 * pair].astype(jnp.float32)
        odd = mixed_ref[2 * pair + 1].astype(jnp.float32)
        for side in range(2):
            here = slice(128 * side, 128 * side + 128)
            e, o = even[:, here], odd[:, here]
            left[2 * side].append(jnp.where(low, e, pltpu.roll(o, COLS, 1)))
            left[2 * side + 1].append(jnp.where(low, pltpu.roll(e, COLS, 1), o))
    left = jnp.concatenate([jnp.concatenate(part, axis=1) for part in left], axis=0)
    left = left.astype(jnp.bfloat16)
    gap = jnp.zeros((128 - YP, 1024), jnp.bfloat16)
    for half, (one, two) in enumerate(((k0_ref, k1_ref), (k2_ref, k3_ref))):
        kernel = jnp.concatenate([one[...], gap, two[...], gap], axis=0)
        crossed = lax.dot_general(
            left, kernel, (((1,), (1,)), ((), ())), preferred_element_type=jnp.float32
        )
        by_day = [crossed[t * rows : (t + 1) * rows] for t in range(DAYS)]
        smooth = []
        for s in range(DAYS):
            total = kt_ref[s, 0] * by_day[0]
            for t in range(1, DAYS):
                total = total + kt_ref[s, t] * by_day[t]
            smooth.append(total)
        smooth = jnp.concatenate(smooth, axis=0).astype(jnp.bfloat16)
        for which in range(2):
            target = (place_ref[2] + 4 - (2 * half + which)) % 4
            out_ref[target] = smooth[:, 128 * which : 128 * which + 128]


def mix_y(place, kt, mixed, pieces):
    return pl.pallas_call(
        mix_y_kernel,
        out_shape=jax.ShapeDtypeStruct((4, DAYS * 2 * XP, 128), jnp.bfloat16),
        in_specs=[pl.BlockSpec(memory_space=pltpu.SMEM)] * 2
        + [pl.BlockSpec(memory_space=pltpu.VMEM)] * 5,
        name="mix_y",
    )(place, kt, mixed, *pieces)


def gather_kernel(count_ref, smooth_ref, cells_ref, fractions_ref, out_ref, window_ref):
    points = out_ref.shape[1]
    rows = PROBES * XP
    days = []
    for s in range(DAYS):
        part = [smooth_ref[source, s * 2 * XP : (s + 1) * 2 * XP, :] for source in range(4)]
        days.append(jnp.concatenate(part, axis=0).astype(jnp.float32))
    blank = jnp.zeros((rows, 128), jnp.float32)
    smooth = [jnp.concatenate([day, blank], axis=1) for day in days]
    for late in range(2):
        window = smooth[late] + pltpu.roll(smooth[late + 1], YP, 1)
        window = window + pltpu.roll(smooth[late + 2], 2 * YP, 1)
        window_ref[late * rows : (late + 1) * rows, :] = window.astype(jnp.bfloat16)

    def step(number, carry):
        start = pl.multiple_of(number * CHUNK, CHUNK)
        where = pl.ds(start, CHUNK)
        x_part, y_days, early, late = point_factors(cells_ref, fractions_ref, where)
        hidden = jnp.dot(window_ref[...], y_days, preferred_element_type=jnp.float32)
        timed = early * hidden[0:rows] + late * hidden[rows : 2 * rows]
        sums = []
        for q in range(PROBES):
            sums.append(
                jnp.sum(timed[q * XP : (q + 1) * XP] * x_part, axis=0, keepdims=True)
            )
        result = jnp.concatenate(sums, axis=0)
        result = jnp.where(live_lanes(count_ref, start, CHUNK), result, 0.0)
        out_ref[:, where] = result.astype(jnp.bfloat16)
        return carry

    lax.fori_loop(0, points // CHUNK, step, 0)


def gather(counts, smooth, cells, fractions):
    rows = PROBES * XP
    return pl.pallas_call(
        gather_kernel,
        out_shape=jax.ShapeDtypeStruct((PROBES, cells.shape[1]), jnp.bfloat16),
        in_specs=[pl.BlockSpec(memory_space=pltpu.SMEM)]
        + [pl.BlockSpec(memory_space=pltpu.VMEM)] * 3,
        scratch_shapes=[pltpu.VMEM((2 * rows, 256), jnp.bfloat16)],
        name="gather",
    )(counts, smooth, cells, fractions)


def up(count):
    return [(i, i + 1) for i in range(count - 1)]


def down(count):
    return [(i + 1, i) for i in range(count - 1)]


def around(kernel, axis, count, rows):
    before = lax.ppermute(kernel[-1:], axis, up(count))
    after = lax.ppermute(kernel[0:2], axis, down(count))
    blank = jnp.zeros((rows - 3 - kernel.shape[0], kernel.shape[1]), kernel.dtype)
    return jnp.concatenate([before, kernel, after, blank], axis=0)


def turns(piece, axis):
    return [piece] + [
        lax.ppermute(piece, axis, [(i, (i + shift) % 4) for i in range(4)]) for shift in (1, 2, 3)
    ]


def body(probes, cells, fractions, counts, kx, ky, kt):
    own = around(kx, GX, 32, XP)
    other = lax.ppermute(own, "c", [(0, 1), (1, 0)])
    pair = jnp.concatenate([own, other], axis=0)
    pair, probes = lax.optimization_barrier((pair, probes))
    kx_pieces = turns(pair, "zl")

    core, low, high = scatter(counts, probes, cells, fractions)
    low = lax.ppermute(low, GY, down(16))
    high = lax.ppermute(high, GY, up(16))
    core, first, last = add_cols(core, low, high)
    first, last, kx_pieces = lax.optimization_barrier((first, last, kx_pieces))
    first = lax.ppermute(first, GX, down(32))
    last = lax.ppermute(last, GX, up(32))
    grid = add_rows(core, first, last)
    grid, ky = lax.optimization_barrier((grid, ky))
    grid = lax.all_to_all(grid, GX, 0, 0, tiled=True)
    ky_pieces = turns(around(ky, GY, 16, YP), "y")
    place = [lax.axis_index(axis) for axis in ("zl", "c", "y")]
    place = jnp.stack(place).astype(jnp.int32)
    grid, ky_pieces, place = lax.optimization_barrier((grid, ky_pieces, place))
    mixed = mix_x(place, grid.reshape(32 * ROWS, 256), kx_pieces)
    mixed = lax.all_to_all(mixed, NEAR, 0, 0, tiled=True)
    mixed = jnp.broadcast_to(mixed.reshape(1, 4, 2 * XP, 256), (4, 4, 2 * XP, 256))
    mixed = lax.all_to_all(mixed.reshape(16, 2 * XP, 256), GY, 0, 0, tiled=True)
    smooth = lax.all_to_all(mix_y(place, kt, mixed, ky_pieces), "y", 0, 0, tiled=True)
    return gather(counts, smooth, cells, fractions)


def solution(mesh):
    fine = Mesh(mesh.devices.reshape(4, 4, 2, 4, 4), AXES)
    return jax.shard_map(
        body,
        mesh=fine,
        in_specs=(
            P(None, AXES),
            P(None, AXES),
            P(None, AXES),
            P(GX, GY),
            P(GX, None),
            P(GY, None),
            P(),
        ),
        out_specs=P(None, AXES),
        check_vma=False,
    )
```

```python
import jax
import jax.numpy as jnp
from jax import lax
from jax.experimental import pallas as pl
from jax.experimental.pallas import tpu as pltpu
from jax.sharding import Mesh
from jax.sharding import PartitionSpec as P

DAYS = 4
PROBES = 8
BLOCK = 128
ROWS = 32
COLS = 64
XP = 40
YP = 80
RIM = 384
CHUNK = 512
AXES = ("zh", "zl", "c", "x", "y")
GX = ("zh", "zl", "c")
NEAR = ("zl", "c")
GY = ("x", "y")
HIGH = lax.Precision.HIGHEST


def keys_weights(fraction):
    first = ((-0.5 * fraction + 1.0) * fraction - 0.5) * fraction
    second = (1.5 * fraction - 2.5) * fraction * fraction + 1.0
    third = ((-1.5 * fraction + 2.0) * fraction + 0.5) * fraction
    fourth = (0.5 * fraction - 0.5) * fraction * fraction
    return (first, second, third, fourth)


def spread(cell, weights, extent):
    row = lax.broadcasted_iota(jnp.int32, (extent, cell.shape[1]), 0) - cell
    result = jnp.where(row == 3, weights[3], 0.0)
    for k in (2, 1, 0):
        result = jnp.where(row == k, weights[k], result)
    return result


def point_factors(cells_ref, fractions_ref, where):
    x_part = spread(
        cells_ref[0:1, where] % ROWS, keys_weights(fractions_ref[0:1, where]), XP
    )
    y_part = spread(
        cells_ref[1:2, where] % COLS, keys_weights(fractions_ref[1:2, where]), YP
    )
    day = cells_ref[2:3, where]
    y_days = [jnp.where(day == d, y_part, 0.0) for d in range(DAYS - 1)]
    y_days.append(jnp.zeros((256 - 3 * YP, y_part.shape[1]), jnp.float32))
    y_days = jnp.concatenate(y_days, axis=0).astype(jnp.bfloat16)
    late = fractions_ref[2:3, where]
    return x_part, y_days, 1.0 - late, late


def live_lanes(count_ref, start, size):
    slot = start + lax.broadcasted_iota(jnp.int32, (1, size), 1)
    return slot // BLOCK < count_ref[0, 0]


def scatter_kernel(
    count_ref, probes_ref, cells_ref, fractions_ref, ky_ref, core_ref, low_ref, high_ref, acc_ref
):
    points = probes_ref.shape[1]
    acc_ref[...] = jnp.zeros_like(acc_ref)

    def step(number, carry):
        start = pl.multiple_of(number * CHUNK, CHUNK)
        where = pl.ds(start, CHUNK)
        x_part, y_days, early, late = point_factors(cells_ref, fractions_ref, where)
        values = jnp.where(
            live_lanes(count_ref, start, CHUNK), probes_ref[:, where].astype(jnp.float32), 0.0
        )
        parts = []
        for weight in (early, late):
            timed = weight * values
            for q in range(PROBES):
                parts.append(timed[q : q + 1] * x_part)
        weighted = jnp.concatenate(parts, axis=0).astype(jnp.bfloat16)
        acc_ref[...] += lax.dot_general(
            weighted, y_days, (((1,), (1,)), ((), ())), preferred_element_type=jnp.float32
        )
        return carry

    lax.fori_loop(0, points // CHUNK, step, 0)
    rows = PROBES * XP
    blank = jnp.zeros((rows, 128), jnp.float32)
    first = jnp.concatenate([acc_ref[0:rows, :], blank], axis=1)
    second = jnp.concatenate([acc_ref[rows : 2 * rows, :], blank], axis=1)
    total = first + pltpu.roll(second, YP, 1)
    lane = lax.broadcasted_iota(jnp.int32, (rows, 384), 1)
    core = pltpu.roll(total, 383, 1)
    for t in range(1, DAYS):
        core = jnp.where(lane // COLS == t, pltpu.roll(total, 384 - (16 * t + 1), 1), core)
    core_ref[...] = core[:, 0:256]
    out_row = lax.broadcasted_iota(jnp.int32, (16, 384), 0)
    in_lane = lax.broadcasted_iota(jnp.int32, (16, 384), 1)
    low = (out_row < DAYS) & (in_lane == YP * out_row)
    high_row = out_row - 8
    high = (high_row >= 0) & (in_lane == YP * (high_row // 2) + (COLS + 1) + high_row % 2)
    pick = jnp.where(low | high, 1.0, 0.0)
    rims = lax.dot_general(
        pick, total, (((1,), (1,)), ((), ())), precision=HIGH, preferred_element_type=jnp.float32
    )
    top = ky_ref[0:16, :].astype(jnp.float32)
    end = ky_ref[COLS - 16 : COLS, :].astype(jnp.float32)
    low_ref[:, 0:rows] = rims[0:8]
    high_ref[:, 0:rows] = rims[8:16]
    for n in range(4):
        here = slice(256 * n, 256 * n + 256)
        for r in range(2):
            low_ref[4 * r + n : 4 * r + n + 1, RIM:] = top[r : r + 1, here]
        high_ref[n : n + 1, RIM:] = end[15:16, here]
    high_ref[4:8, RIM:] = jnp.zeros((4, 256), jnp.float32)
    low_ref[:, rows:RIM] = jnp.zeros((8, RIM - rows), jnp.float32)
    high_ref[:, rows:RIM] = jnp.zeros((8, RIM - rows), jnp.float32)


def scatter(counts, probes, cells, fractions, ky):
    rows = PROBES * XP
    return pl.pallas_call(
        scatter_kernel,
        out_shape=(
            jax.ShapeDtypeStruct((rows, 256), jnp.float32),
            jax.ShapeDtypeStruct((8, RIM + 256), jnp.float32),
            jax.ShapeDtypeStruct((8, RIM + 256), jnp.float32),
        ),
        in_specs=[pl.BlockSpec(memory_space=pltpu.SMEM)]
        + [pl.BlockSpec(memory_space=pltpu.VMEM)] * 4,
        scratch_shapes=[pltpu.VMEM((2 * rows, 256), jnp.float32)],
        name="scatter",
    )(counts, probes, cells, fractions, ky)


def add_cols_kernel(core_ref, low_ref, high_ref, out_ref, first_ref, last_ref):
    row = lax.broadcasted_iota(jnp.int32, (16, 256), 0)
    lane = lax.broadcasted_iota(jnp.int32, (16, 256), 1)
    high_row = row - 8
    put = (row < DAYS) & (lane == COLS * row + (COLS - 1))
    put = put | ((high_row >= 0) & (lane == COLS * (high_row // 2) + high_row % 2))
    width = core_ref.shape[0]
    received = jnp.concatenate([low_ref[:, 0:width], high_ref[:, 0:width]], axis=0)
    out_ref[...] = core_ref[...] + lax.dot_general(
        received,
        jnp.where(put, 1.0, 0.0),
        (((0,), (0,)), ((), ())),
        precision=HIGH,
        preferred_element_type=jnp.float32,
    )
    first, last = [], []
    for q in range(PROBES):
        first.append(out_ref[q * XP : q * XP + 1, :])
        last.append(out_ref[q * XP + ROWS + 1 : q * XP + ROWS + 3, :])
    first_ref[...] = jnp.concatenate(first, axis=0)
    last_ref[...] = jnp.concatenate(last, axis=0)


def add_cols(core, low, high):
    return pl.pallas_call(
        add_cols_kernel,
        out_shape=(
            jax.ShapeDtypeStruct(core.shape, jnp.float32),
            jax.ShapeDtypeStruct((PROBES, 256), jnp.float32),
            jax.ShapeDtypeStruct((2 * PROBES, 256), jnp.float32),
        ),
        name="add_cols",
    )(core, low, high)


def add_rows_kernel(core_ref, first_ref, last_ref, out_ref):
    row = lax.broadcasted_iota(jnp.int32, (ROWS, 256), 0)
    for q in range(PROBES):
        tile = core_ref[q * XP + 1 : q * XP + 1 + ROWS, :]
        extra = jnp.where(row == ROWS - 1, first_ref[q : q + 1, :], 0.0)
        extra = jnp.where(row == 0, last_ref[2 * q : 2 * q + 1, :], extra)
        extra = jnp.where(row == 1, last_ref[2 * q + 1 : 2 * q + 2, :], extra)
        tile = (tile + extra).astype(jnp.bfloat16)
        for copy in range(4):
            out_ref[copy * PROBES + q] = tile


def add_rows(core, first, last):
    return pl.pallas_call(
        add_rows_kernel,
        out_shape=jax.ShapeDtypeStruct((4 * PROBES, ROWS, 256), jnp.bfloat16),
        name="add_rows",
    )(core, first, last)


def mix_x_kernel(grid_ref, kernel_ref, before_ref, after_ref, out_ref, rows_ref):
    blank = jnp.zeros((5, 1024), jnp.float32)
    outer = [after_ref[...].astype(jnp.float32), blank, before_ref[...].astype(jnp.float32)]
    outer = jnp.concatenate(outer, axis=0).astype(jnp.bfloat16)
    outer = jnp.dot(outer, grid_ref[...], preferred_element_type=jnp.float32)
    rows_ref[0:8, :] = outer
    rows_ref[264:272, :] = outer
    rows_ref[8:264, :] = jnp.dot(
        kernel_ref[...], grid_ref[...], preferred_element_type=jnp.float32
    )
    for tile in range(8):
        out_ref[tile] = rows_ref[7 + ROWS * tile : 7 + ROWS * tile + XP, :].astype(jnp.bfloat16)


def mix_x(grid, kernel, before, after):
    return pl.pallas_call(
        mix_x_kernel,
        out_shape=jax.ShapeDtypeStruct((8, XP, 256), jnp.bfloat16),
        scratch_shapes=[pltpu.VMEM((272, 256), jnp.float32)],
        name="mix_x",
    )(grid, kernel, before, after)


def mix_y_kernel(place_ref, kt_ref, mixed_ref, k0_ref, k1_ref, k2_ref, k3_ref, out_ref):
    rows = 2 * XP
    low = lax.broadcasted_iota(jnp.int32, (rows, 128), 1) < COLS
    left = [[] for _ in range(DAYS)]
    for pair in range(8):
        even = mixed_ref[2 * pair].astype(jnp.float32)
        odd = mixed_ref[2 * pair + 1].astype(jnp.float32)
        for side in range(2):
            here = slice(128 * side, 128 * side + 128)
            e, o = even[:, here], odd[:, here]
            left[2 * side].append(jnp.where(low, e, pltpu.roll(o, COLS, 1)))
            left[2 * side + 1].append(jnp.where(low, pltpu.roll(e, COLS, 1), o))
    left = jnp.concatenate([jnp.concatenate(part, axis=1) for part in left], axis=0)
    left = left.astype(jnp.bfloat16)
    gap = jnp.zeros((128 - YP, 1024), jnp.bfloat16)
    for half, (one, two) in enumerate(((k0_ref, k1_ref), (k2_ref, k3_ref))):
        kernel = jnp.concatenate([one[...], gap, two[...], gap], axis=0)
        crossed = lax.dot_general(
            left, kernel, (((1,), (1,)), ((), ())), preferred_element_type=jnp.float32
        )
        by_day = [crossed[t * rows : (t + 1) * rows] for t in range(DAYS)]
        smooth = []
        for s in range(DAYS):
            total = kt_ref[s, 0] * by_day[0]
            for t in range(1, DAYS):
                total = total + kt_ref[s, t] * by_day[t]
            smooth.append(total)
        smooth = jnp.concatenate(smooth, axis=0).astype(jnp.bfloat16)
        for which in range(2):
            target = (place_ref[0] + 4 - (2 * half + which)) % 4
            out_ref[target] = smooth[:, 128 * which : 128 * which + 128]


def mix_y(place, kt, mixed, pieces):
    return pl.pallas_call(
        mix_y_kernel,
        out_shape=jax.ShapeDtypeStruct((4, DAYS * 2 * XP, 128), jnp.bfloat16),
        in_specs=[pl.BlockSpec(memory_space=pltpu.SMEM)] * 2
        + [pl.BlockSpec(memory_space=pltpu.VMEM)] * 5,
        name="mix_y",
    )(place, kt, mixed, *pieces)


def gather_kernel(count_ref, smooth_ref, cells_ref, fractions_ref, out_ref, window_ref):
    points = out_ref.shape[1]
    rows = PROBES * XP
    days = []
    for s in range(DAYS):
        part = [smooth_ref[source, s * 2 * XP : (s + 1) * 2 * XP, :] for source in range(4)]
        days.append(jnp.concatenate(part, axis=0).astype(jnp.float32))
    blank = jnp.zeros((rows, 128), jnp.float32)
    smooth = [jnp.concatenate([day, blank], axis=1) for day in days]
    for late in range(2):
        window = smooth[late] + pltpu.roll(smooth[late + 1], YP, 1)
        window = window + pltpu.roll(smooth[late + 2], 2 * YP, 1)
        window_ref[late * rows : (late + 1) * rows, :] = window.astype(jnp.bfloat16)

    def step(number, carry):
        start = pl.multiple_of(number * CHUNK, CHUNK)
        where = pl.ds(start, CHUNK)
        x_part, y_days, early, late = point_factors(cells_ref, fractions_ref, where)
        hidden = jnp.dot(window_ref[...], y_days, preferred_element_type=jnp.float32)
        timed = early * hidden[0:rows] + late * hidden[rows : 2 * rows]
        sums = []
        for q in range(PROBES):
            sums.append(
                jnp.sum(timed[q * XP : (q + 1) * XP] * x_part, axis=0, keepdims=True)
            )
        result = jnp.concatenate(sums, axis=0)
        result = jnp.where(live_lanes(count_ref, start, CHUNK), result, 0.0)
        out_ref[:, where] = result.astype(jnp.bfloat16)
        return carry

    lax.fori_loop(0, points // CHUNK, step, 0)


def gather(counts, smooth, cells, fractions):
    rows = PROBES * XP
    return pl.pallas_call(
        gather_kernel,
        out_shape=jax.ShapeDtypeStruct((PROBES, cells.shape[1]), jnp.bfloat16),
        in_specs=[pl.BlockSpec(memory_space=pltpu.SMEM)]
        + [pl.BlockSpec(memory_space=pltpu.VMEM)] * 3,
        scratch_shapes=[pltpu.VMEM((2 * rows, 256), jnp.bfloat16)],
        name="gather",
    )(counts, smooth, cells, fractions)


def up(count):
    return [(i, i + 1) for i in range(count - 1)]


def down(count):
    return [(i + 1, i) for i in range(count - 1)]


def turns(piece, axis):
    return [piece] + [
        lax.ppermute(piece, axis, [(i, (i + shift) % 4) for i in range(4)]) for shift in (1, 2, 3)
    ]


def body(probes, cells, fractions, counts, kx, ky, kt):
    kernel = jnp.broadcast_to(kx[None], (8,) + kx.shape)
    kernel = lax.all_to_all(kernel, NEAR, 0, 0, tiled=True).reshape(8 * ROWS, 1024)
    core, low, high = scatter(counts, probes, cells, fractions, ky)
    low, kernel = lax.optimization_barrier((low, kernel))
    low = lax.ppermute(low, GY, down(16))
    high = lax.ppermute(high, GY, up(16))
    core, first, last = add_cols(core, low, high)
    first = lax.ppermute(first, GX, down(32))
    last = lax.ppermute(last, GX, up(32))
    grid = add_rows(core, first, last)
    grid, ky, kernel = lax.optimization_barrier((grid, ky, kernel))
    grid = lax.all_to_all(grid, GX, 0, 0, tiled=True)
    before = lax.ppermute(kernel[8 * ROWS - 1 :], "zh", up(4))
    after = lax.ppermute(kernel[0:2], "zh", down(4))
    right = low[:, RIM:].reshape(2, 1024).astype(ky.dtype)
    left = high[0:4, RIM:].reshape(1, 1024).astype(ky.dtype)
    blank = jnp.zeros((YP - COLS - 3, 1024), ky.dtype)
    ky_pieces = turns(jnp.concatenate([left, ky, right, blank], axis=0), "y")
    place = lax.axis_index("y").astype(jnp.int32).reshape(1)
    rest = (grid, ky_pieces, place, before, after)
    grid, ky_pieces, place, before, after = lax.optimization_barrier(rest)
    mixed = mix_x(grid.reshape(32 * ROWS, 256), kernel, before, after)
    mixed = lax.all_to_all(mixed, NEAR, 0, 0, tiled=True)
    mixed = jnp.broadcast_to(mixed.reshape(1, 4, 2 * XP, 256), (4, 4, 2 * XP, 256))
    mixed = lax.all_to_all(mixed.reshape(16, 2 * XP, 256), GY, 0, 0, tiled=True)
    smooth = lax.all_to_all(mix_y(place, kt, mixed, ky_pieces), "y", 0, 0, tiled=True)
    return gather(counts, smooth, cells, fractions)


def solution(mesh):
    fine = Mesh(mesh.devices.reshape(4, 4, 2, 4, 4), AXES)
    return jax.shard_map(
        body,
        mesh=fine,
        in_specs=(
            P(None, AXES),
            P(None, AXES),
            P(None, AXES),
            P(GX, GY),
            P(GX, None),
            P(GY, None),
            P(),
        ),
        out_specs=P(None, AXES),
        check_vma=False,
    )
```

```python
import jax
import jax.numpy as jnp
from jax import lax
from jax.experimental import pallas as pl
from jax.experimental.pallas import tpu as pltpu
from jax.sharding import Mesh
from jax.sharding import PartitionSpec as P

DAYS = 4
PROBES = 8
BLOCK = 128
ROWS = 32
COLS = 64
XP = 40
PART = 9
STEP = 10
YP = 80
RIM = 384
CHUNK = 512
AXES = ("zh", "zl", "c", "x", "y")
GX = ("zh", "zl", "c")
NEAR = ("zl", "c")
HOME = ("zl", "c", "y")
GY = ("x", "y")
HIGH = lax.Precision.HIGHEST


def keys_weights(fraction):
    first = ((-0.5 * fraction + 1.0) * fraction - 0.5) * fraction
    second = (1.5 * fraction - 2.5) * fraction * fraction + 1.0
    third = ((-1.5 * fraction + 2.0) * fraction + 0.5) * fraction
    fourth = (0.5 * fraction - 0.5) * fraction * fraction
    return (first, second, third, fourth)


def spread(cell, weights, row):
    row = row - cell
    result = jnp.where(row == 3, weights[3], 0.0)
    for k in (2, 1, 0):
        result = jnp.where(row == k, weights[k], result)
    return result


def point_factors(cells_ref, fractions_ref, where, row):
    col = lax.broadcasted_iota(jnp.int32, (YP, CHUNK), 0)
    x_part = spread(cells_ref[0:1, where] % ROWS, keys_weights(fractions_ref[0:1, where]), row)
    y_part = spread(cells_ref[1:2, where] % COLS, keys_weights(fractions_ref[1:2, where]), col)
    day = cells_ref[2:3, where]
    y_days = [jnp.where(day == d, y_part, 0.0) for d in range(DAYS - 1)]
    y_days.append(jnp.zeros((256 - 3 * YP, y_part.shape[1]), jnp.float32))
    y_days = jnp.concatenate(y_days, axis=0).astype(jnp.bfloat16)
    late = fractions_ref[2:3, where]
    return x_part, y_days, 1.0 - late, late


def live_lanes(count_ref, start, size):
    slot = start + lax.broadcasted_iota(jnp.int32, (1, size), 1)
    return slot // BLOCK < count_ref[0, 0]


def scatter_kernel(
    count_ref, probes_ref, cells_ref, fractions_ref, ky_ref, core_ref, low_ref, high_ref, acc_ref
):
    points = probes_ref.shape[1]
    acc_ref[...] = jnp.zeros_like(acc_ref)

    def step(number, carry):
        start = pl.multiple_of(number * CHUNK, CHUNK)
        where = pl.ds(start, CHUNK)
        row = lax.broadcasted_iota(jnp.int32, (XP, CHUNK), 0)
        x_part, y_days, early, late = point_factors(cells_ref, fractions_ref, where, row)
        values = jnp.where(
            live_lanes(count_ref, start, CHUNK), probes_ref[:, where].astype(jnp.float32), 0.0
        )
        parts = []
        for weight in (early, late):
            timed = weight * values
            for q in range(PROBES):
                parts.append(timed[q : q + 1] * x_part)
        weighted = jnp.concatenate(parts, axis=0).astype(jnp.bfloat16)
        acc_ref[...] += lax.dot_general(
            weighted, y_days, (((1,), (1,)), ((), ())), preferred_element_type=jnp.float32
        )
        return carry

    lax.fori_loop(0, points // CHUNK, step, 0)
    rows = PROBES * XP
    blank = jnp.zeros((rows, 128), jnp.float32)
    first = jnp.concatenate([acc_ref[0:rows, :], blank], axis=1)
    second = jnp.concatenate([acc_ref[rows : 2 * rows, :], blank], axis=1)
    total = first + pltpu.roll(second, YP, 1)
    lane = lax.broadcasted_iota(jnp.int32, (rows, 384), 1)
    core = pltpu.roll(total, 383, 1)
    for t in range(1, DAYS):
        core = jnp.where(lane // COLS == t, pltpu.roll(total, 384 - (16 * t + 1), 1), core)
    core_ref[...] = core[:, 0:256]
    out_row = lax.broadcasted_iota(jnp.int32, (16, 384), 0)
    in_lane = lax.broadcasted_iota(jnp.int32, (16, 384), 1)
    low = (out_row < DAYS) & (in_lane == YP * out_row)
    high_row = out_row - 8
    high = (high_row >= 0) & (in_lane == YP * (high_row // 2) + (COLS + 1) + high_row % 2)
    pick = jnp.where(low | high, 1.0, 0.0)
    rims = lax.dot_general(
        pick, total, (((1,), (1,)), ((), ())), precision=HIGH, preferred_element_type=jnp.float32
    )
    top = ky_ref[0:16, :].astype(jnp.float32)
    end = ky_ref[COLS - 16 : COLS, :].astype(jnp.float32)
    low_ref[:, 0:rows] = rims[0:8]
    high_ref[:, 0:rows] = rims[8:16]
    for n in range(4):
        here = slice(256 * n, 256 * n + 256)
        for r in range(2):
            low_ref[4 * r + n : 4 * r + n + 1, RIM:] = top[r : r + 1, here]
        high_ref[n : n + 1, RIM:] = end[15:16, here]
    high_ref[4:8, RIM:] = jnp.zeros((4, 256), jnp.float32)
    low_ref[:, rows:RIM] = jnp.zeros((8, RIM - rows), jnp.float32)
    high_ref[:, rows:RIM] = jnp.zeros((8, RIM - rows), jnp.float32)


def scatter(counts, probes, cells, fractions, ky):
    rows = PROBES * XP
    return pl.pallas_call(
        scatter_kernel,
        out_shape=(
            jax.ShapeDtypeStruct((rows, 256), jnp.float32),
            jax.ShapeDtypeStruct((8, RIM + 256), jnp.float32),
            jax.ShapeDtypeStruct((8, RIM + 256), jnp.float32),
        ),
        in_specs=[pl.BlockSpec(memory_space=pltpu.SMEM)]
        + [pl.BlockSpec(memory_space=pltpu.VMEM)] * 4,
        scratch_shapes=[pltpu.VMEM((2 * rows, 256), jnp.float32)],
        name="scatter",
    )(counts, probes, cells, fractions, ky)


def add_cols_kernel(core_ref, low_ref, high_ref, out_ref, first_ref, last_ref):
    row = lax.broadcasted_iota(jnp.int32, (16, 256), 0)
    lane = lax.broadcasted_iota(jnp.int32, (16, 256), 1)
    high_row = row - 8
    put = (row < DAYS) & (lane == COLS * row + (COLS - 1))
    put = put | ((high_row >= 0) & (lane == COLS * (high_row // 2) + high_row % 2))
    width = core_ref.shape[0]
    received = jnp.concatenate([low_ref[:, 0:width], high_ref[:, 0:width]], axis=0)
    out_ref[...] = core_ref[...] + lax.dot_general(
        received,
        jnp.where(put, 1.0, 0.0),
        (((0,), (0,)), ((), ())),
        precision=HIGH,
        preferred_element_type=jnp.float32,
    )
    first, last = [], []
    for q in range(PROBES):
        first.append(out_ref[q * XP : q * XP + 1, :])
        last.append(out_ref[q * XP + ROWS + 1 : q * XP + ROWS + 3, :])
    first_ref[...] = jnp.concatenate(first, axis=0)
    last_ref[...] = jnp.concatenate(last, axis=0)


def add_cols(core, low, high):
    return pl.pallas_call(
        add_cols_kernel,
        out_shape=(
            jax.ShapeDtypeStruct(core.shape, jnp.float32),
            jax.ShapeDtypeStruct((PROBES, 256), jnp.float32),
            jax.ShapeDtypeStruct((2 * PROBES, 256), jnp.float32),
        ),
        name="add_cols",
    )(core, low, high)


def add_rows_kernel(core_ref, first_ref, last_ref, out_ref):
    row = lax.broadcasted_iota(jnp.int32, (ROWS, 256), 0)
    for q in range(PROBES):
        tile = core_ref[q * XP + 1 : q * XP + 1 + ROWS, :]
        extra = jnp.where(row == ROWS - 1, first_ref[q : q + 1, :], 0.0)
        extra = jnp.where(row == 0, last_ref[2 * q : 2 * q + 1, :], extra)
        extra = jnp.where(row == 1, last_ref[2 * q + 1 : 2 * q + 2, :], extra)
        tile = (tile + extra).astype(jnp.bfloat16)
        for copy in range(4):
            out_ref[copy * PROBES + q] = tile


def add_rows(core, first, last):
    return pl.pallas_call(
        add_rows_kernel,
        out_shape=jax.ShapeDtypeStruct((4 * PROBES, ROWS, 256), jnp.bfloat16),
        name="add_rows",
    )(core, first, last)


def mix_x_kernel(grid_ref, kernel_ref, before_ref, after_ref, out_ref, rows_ref):
    blank = jnp.zeros((5, 1024), jnp.float32)
    outer = [after_ref[...].astype(jnp.float32), blank, before_ref[...].astype(jnp.float32)]
    outer = jnp.concatenate(outer, axis=0).astype(jnp.bfloat16)
    outer = jnp.dot(outer, grid_ref[...], preferred_element_type=jnp.float32)
    inner = jnp.dot(kernel_ref[...], grid_ref[...], preferred_element_type=jnp.float32)
    for side in range(2):
        here = slice(128 * side, 128 * side + 128)
        rows_ref[side, 0:8, :] = outer[:, here]
        rows_ref[side, 264:272, :] = outer[:, here]
        rows_ref[side, 8:264, :] = inner[:, here]
    for part in range(4):
        rows = []
        for r in range(STEP):
            start = 7 + PART * part + r
            wide = [rows_ref[side, pl.ds(start, 8, stride=ROWS), :] for side in range(2)]
            rows.append(jnp.concatenate(wide, axis=1))
        out_ref[part] = jnp.concatenate(rows, axis=0).astype(jnp.bfloat16)


def mix_x(grid, kernel, before, after):
    return pl.pallas_call(
        mix_x_kernel,
        out_shape=jax.ShapeDtypeStruct((4, 8 * STEP, 256), jnp.bfloat16),
        scratch_shapes=[pltpu.VMEM((2, 272, 128), jnp.float32)],
        name="mix_x",
    )(grid, kernel, before, after)


def mix_y_kernel(
    place_ref, kt_ref, mixed_ref, k0_ref, k1_ref, k2_ref, k3_ref, out_ref, smooth_ref
):
    rows = 8 * STEP
    low = lax.broadcasted_iota(jnp.int32, (rows, 128), 1) < COLS
    left = [[] for _ in range(DAYS)]
    for pair in range(8):
        even = mixed_ref[2 * pair].astype(jnp.float32)
        odd = mixed_ref[2 * pair + 1].astype(jnp.float32)
        for side in range(2):
            here = slice(128 * side, 128 * side + 128)
            e, o = even[:, here], odd[:, here]
            left[2 * side].append(jnp.where(low, e, pltpu.roll(o, COLS, 1)))
            left[2 * side + 1].append(jnp.where(low, pltpu.roll(e, COLS, 1), o))
    left = jnp.concatenate([jnp.concatenate(part, axis=1) for part in left], axis=0)
    left = left.astype(jnp.bfloat16)
    gap = jnp.zeros((128 - YP, 1024), jnp.bfloat16)
    for half, (one, two) in enumerate(((k0_ref, k1_ref), (k2_ref, k3_ref))):
        kernel = jnp.concatenate([one[...], gap, two[...], gap], axis=0)
        crossed = lax.dot_general(
            left, kernel, (((1,), (1,)), ((), ())), preferred_element_type=jnp.float32
        )
        by_day = [crossed[t * rows : (t + 1) * rows] for t in range(DAYS)]
        for s in range(DAYS):
            total = kt_ref[s, 0] * by_day[0]
            for t in range(1, DAYS):
                total = total + kt_ref[s, t] * by_day[t]
            for which in range(2):
                here = slice(128 * which, 128 * which + 128)
                smooth_ref[which, s * rows : (s + 1) * rows, :] = total[:, here]
        for which in range(2):
            target = (place_ref[0] + 4 - (2 * half + which)) % 4
            for tile in range(8):
                part = smooth_ref[which, pl.ds(tile, DAYS * STEP, stride=8), :]
                out_ref[tile, target] = part.astype(jnp.bfloat16)


def mix_y(place, kt, mixed, pieces):
    return pl.pallas_call(
        mix_y_kernel,
        out_shape=jax.ShapeDtypeStruct((8, 4, DAYS * STEP, 128), jnp.bfloat16),
        in_specs=[pl.BlockSpec(memory_space=pltpu.SMEM)] * 2
        + [pl.BlockSpec(memory_space=pltpu.VMEM)] * 5,
        scratch_shapes=[pltpu.VMEM((2, DAYS * 8 * STEP, 128), jnp.float32)],
        name="mix_y",
    )(place, kt, mixed, *pieces)


def gather_kernel(
    count_ref, smooth_ref, cells_ref, fractions_ref, out_ref, wide_ref, window_ref, sums_ref
):
    points = out_ref.shape[1]
    rows = STEP * 4 * PROBES
    wide_ref[...] = smooth_ref[...].astype(jnp.float32)
    days = []
    for s in range(DAYS):
        part = [
            wide_ref[pl.ds(s * STEP + r, 4 * PROBES, stride=DAYS * STEP), :] for r in range(STEP)
        ]
        days.append(jnp.concatenate(part, axis=0))
    blank = jnp.zeros((rows, 128), jnp.float32)
    smooth = [jnp.concatenate([day, blank], axis=1) for day in days]
    for late in range(2):
        window = smooth[late] + pltpu.roll(smooth[late + 1], YP, 1)
        window = window + pltpu.roll(smooth[late + 2], 2 * YP, 1)
        window_ref[late * rows : (late + 1) * rows, :] = window.astype(jnp.bfloat16)

    def step(number, carry):
        start = pl.multiple_of(number * CHUNK, CHUNK)
        where = pl.ds(start, CHUNK)
        row = lax.broadcasted_iota(jnp.int32, (8 * STEP, CHUNK), 0)
        row = jnp.where(row // 8 < PART, PART * (row % 4) + row // 8, 8 * XP)
        x_part, y_days, early, late = point_factors(cells_ref, fractions_ref, where, row)
        hidden = jnp.dot(window_ref[...], y_days, preferred_element_type=jnp.float32)
        total = jnp.zeros((4 * PROBES, CHUNK), jnp.float32)
        for r in range(STEP):
            here = slice(r * 4 * PROBES, (r + 1) * 4 * PROBES)
            timed = early * hidden[here] + late * hidden[rows + here.start : rows + here.stop]
            factor = x_part[8 * r : 8 * r + 8]
            total += timed * jnp.concatenate([factor] * 4, axis=0)
        result = jnp.zeros((PROBES, CHUNK), jnp.float32)
        for side in range(CHUNK // 128):
            sums_ref[side] = total[:, 128 * side : 128 * side + 128]
        for part in range(4):
            piece = [
                sums_ref[side, pl.ds(part, PROBES, stride=4), :] for side in range(CHUNK // 128)
            ]
            result += jnp.concatenate(piece, axis=1)
        result = jnp.where(live_lanes(count_ref, start, CHUNK), result, 0.0)
        out_ref[:, where] = result.astype(jnp.bfloat16)
        return carry

    lax.fori_loop(0, points // CHUNK, step, 0)


def gather(counts, smooth, cells, fractions):
    rows = STEP * 4 * PROBES
    return pl.pallas_call(
        gather_kernel,
        out_shape=jax.ShapeDtypeStruct((PROBES, cells.shape[1]), jnp.bfloat16),
        in_specs=[pl.BlockSpec(memory_space=pltpu.SMEM)]
        + [pl.BlockSpec(memory_space=pltpu.VMEM)] * 3,
        scratch_shapes=[
            pltpu.VMEM((DAYS * rows, 128), jnp.float32),
            pltpu.VMEM((2 * rows, 256), jnp.bfloat16),
            pltpu.VMEM((CHUNK // 128, 4 * PROBES, 128), jnp.float32),
        ],
        name="gather",
    )(counts, smooth, cells, fractions)


def up(count):
    return [(i, i + 1) for i in range(count - 1)]


def down(count):
    return [(i + 1, i) for i in range(count - 1)]


def turns(piece, axis):
    return [piece] + [
        lax.ppermute(piece, axis, [(i, (i + shift) % 4) for i in range(4)]) for shift in (1, 2, 3)
    ]


def body(probes, cells, fractions, counts, kx, ky, kt):
    kernel = jnp.broadcast_to(kx[None], (8,) + kx.shape)
    kernel = lax.all_to_all(kernel, NEAR, 0, 0, tiled=True).reshape(8 * ROWS, 1024)
    core, low, high = scatter(counts, probes, cells, fractions, ky)
    low = lax.ppermute(low, GY, down(16))
    high = lax.ppermute(high, GY, up(16))
    core, first, last = add_cols(core, low, high)
    first, last, kernel = lax.optimization_barrier((first, last, kernel))
    first = lax.ppermute(first, GX, down(32))
    last = lax.ppermute(last, GX, up(32))
    grid = add_rows(core, first, last)
    grid, ky, kernel = lax.optimization_barrier((grid, ky, kernel))
    grid = lax.all_to_all(grid, GX, 0, 0, tiled=True)
    before = lax.ppermute(kernel[8 * ROWS - 1 :], "zh", up(4))
    after = lax.ppermute(kernel[0:2], "zh", down(4))
    right = low[:, RIM:].reshape(2, 1024).astype(ky.dtype)
    left = high[0:4, RIM:].reshape(1, 1024).astype(ky.dtype)
    blank = jnp.zeros((YP - COLS - 3, 1024), ky.dtype)
    ky_pieces = turns(jnp.concatenate([left, ky, right, blank], axis=0), "y")
    place = lax.axis_index("y").astype(jnp.int32).reshape(1)
    rest = (grid, ky_pieces, place, before, after)
    grid, ky_pieces, place, before, after = lax.optimization_barrier(rest)
    mixed = mix_x(grid.reshape(32 * ROWS, 256), kernel, before, after)
    mixed = jnp.broadcast_to(mixed[None], (4,) + mixed.shape)
    mixed = lax.all_to_all(mixed.reshape(16, 8 * STEP, 256), GY, 0, 0, tiled=True)
    smooth = mix_y(place, kt, mixed, ky_pieces).reshape(32, DAYS * STEP, 128)
    smooth = lax.all_to_all(smooth, HOME, 0, 0, tiled=True)
    return gather(counts, smooth.reshape(32 * DAYS * STEP, 128), cells, fractions)


def solution(mesh):
    fine = Mesh(mesh.devices.reshape(4, 4, 2, 4, 4), AXES)
    return jax.shard_map(
        body,
        mesh=fine,
        in_specs=(
            P(None, AXES),
            P(None, AXES),
            P(None, AXES),
            P(GX, GY),
            P(GX, None),
            P(GY, None),
            P(),
        ),
        out_specs=P(None, AXES),
        check_vma=False,
    )
```

```python
import jax
import jax.numpy as jnp
from jax import lax
from jax.experimental import pallas as pl
from jax.experimental.pallas import tpu as pltpu
from jax.sharding import Mesh
from jax.sharding import PartitionSpec as P

DAYS = 4
PROBES = 8
BLOCK = 128
ROWS = 32
COLS = 64
XP = 40
PART = 9
STEP = 10
YP = 80
RIM = 384
CHUNK = 512
AXES = ("zh", "zl", "c", "x", "y")
GX = ("zh", "zl", "c")
NEAR = ("zl", "c")
HOME = ("zl", "c", "y")
GY = ("x", "y")
HIGH = lax.Precision.HIGHEST


def near(*arrays):
    return [pltpu.with_memory_space_constraint(array, pltpu.VMEM) for array in arrays]


def keys_weights(fraction):
    first = ((-0.5 * fraction + 1.0) * fraction - 0.5) * fraction
    second = (1.5 * fraction - 2.5) * fraction * fraction + 1.0
    third = ((-1.5 * fraction + 2.0) * fraction + 0.5) * fraction
    fourth = (0.5 * fraction - 0.5) * fraction * fraction
    return (first, second, third, fourth)


def spread(cell, weights, row):
    row = row - cell
    result = jnp.where(row == 3, weights[3], 0.0)
    for k in (2, 1, 0):
        result = jnp.where(row == k, weights[k], result)
    return result


def point_factors(cells_ref, fractions_ref, where, row):
    col = lax.broadcasted_iota(jnp.int32, (YP, CHUNK), 0)
    x_part = spread(cells_ref[0:1, where] % ROWS, keys_weights(fractions_ref[0:1, where]), row)
    y_part = spread(cells_ref[1:2, where] % COLS, keys_weights(fractions_ref[1:2, where]), col)
    day = cells_ref[2:3, where]
    y_days = [jnp.where(day == d, y_part, 0.0) for d in range(DAYS - 1)]
    y_days.append(jnp.zeros((256 - 3 * YP, y_part.shape[1]), jnp.float32))
    y_days = jnp.concatenate(y_days, axis=0).astype(jnp.bfloat16)
    late = fractions_ref[2:3, where]
    return x_part, y_days, 1.0 - late, late


def live_lanes(count_ref, start, size):
    slot = start + lax.broadcasted_iota(jnp.int32, (1, size), 1)
    return slot // BLOCK < count_ref[0, 0]


def scatter_kernel(
    count_ref,
    probes_ref,
    cells_ref,
    fractions_ref,
    ky_ref,
    core_ref,
    low_ref,
    high_ref,
    acc_ref,
    left0_ref,
    left1_ref,
    right0_ref,
    right1_ref,
):
    chunks = probes_ref.shape[1] // CHUNK
    acc_ref[...] = jnp.zeros_like(acc_ref)

    def prepare(number, left_ref, right_ref):
        start = pl.multiple_of(number * CHUNK, CHUNK)
        where = pl.ds(start, CHUNK)
        row = lax.broadcasted_iota(jnp.int32, (XP, CHUNK), 0)
        x_part, y_days, early, late = point_factors(cells_ref, fractions_ref, where, row)
        values = jnp.where(
            live_lanes(count_ref, start, CHUNK), probes_ref[:, where].astype(jnp.float32), 0.0
        )
        parts = []
        for weight in (early, late):
            timed = weight * values
            for q in range(PROBES):
                parts.append(timed[q : q + 1] * x_part)
        left_ref[...] = jnp.concatenate(parts, axis=0).astype(jnp.bfloat16)
        right_ref[...] = y_days

    def product(left_ref, right_ref):
        acc_ref[...] += lax.dot_general(
            left_ref[...],
            right_ref[...],
            (((1,), (1,)), ((), ())),
            preferred_element_type=jnp.float32,
        )

    def step(number, carry):
        product(left0_ref, right0_ref)
        prepare(2 * number + 1, left1_ref, right1_ref)
        product(left1_ref, right1_ref)
        prepare(jnp.minimum(2 * number + 2, chunks - 1), left0_ref, right0_ref)
        return carry

    prepare(0, left0_ref, right0_ref)
    lax.fori_loop(0, chunks // 2, step, 0)
    rows = PROBES * XP
    blank = jnp.zeros((rows, 128), jnp.float32)
    first = jnp.concatenate([acc_ref[0:rows, :], blank], axis=1)
    second = jnp.concatenate([acc_ref[rows : 2 * rows, :], blank], axis=1)
    total = first + pltpu.roll(second, YP, 1)
    lane = lax.broadcasted_iota(jnp.int32, (rows, 384), 1)
    core = pltpu.roll(total, 383, 1)
    for t in range(1, DAYS):
        core = jnp.where(lane // COLS == t, pltpu.roll(total, 384 - (16 * t + 1), 1), core)
    core_ref[...] = core[:, 0:256]
    out_row = lax.broadcasted_iota(jnp.int32, (16, 384), 0)
    in_lane = lax.broadcasted_iota(jnp.int32, (16, 384), 1)
    low = (out_row < DAYS) & (in_lane == YP * out_row)
    high_row = out_row - 8
    high = (high_row >= 0) & (in_lane == YP * (high_row // 2) + (COLS + 1) + high_row % 2)
    pick = jnp.where(low | high, 1.0, 0.0)
    rims = lax.dot_general(
        pick, total, (((1,), (1,)), ((), ())), precision=HIGH, preferred_element_type=jnp.float32
    )
    top = ky_ref[0:16, :].astype(jnp.float32)
    end = ky_ref[COLS - 16 : COLS, :].astype(jnp.float32)
    low_ref[:, 0:rows] = rims[0:8]
    high_ref[:, 0:rows] = rims[8:16]
    for n in range(4):
        here = slice(256 * n, 256 * n + 256)
        for r in range(2):
            low_ref[4 * r + n : 4 * r + n + 1, RIM:] = top[r : r + 1, here]
        high_ref[n : n + 1, RIM:] = end[15:16, here]
    high_ref[4:8, RIM:] = jnp.zeros((4, 256), jnp.float32)
    low_ref[:, rows:RIM] = jnp.zeros((8, RIM - rows), jnp.float32)
    high_ref[:, rows:RIM] = jnp.zeros((8, RIM - rows), jnp.float32)


def scatter(counts, probes, cells, fractions, ky):
    rows = PROBES * XP
    return pl.pallas_call(
        scatter_kernel,
        out_shape=(
            pltpu.VMEM((rows, 256), jnp.float32),
            pltpu.VMEM((8, RIM + 256), jnp.float32),
            pltpu.VMEM((8, RIM + 256), jnp.float32),
        ),
        in_specs=[pl.BlockSpec(memory_space=pltpu.SMEM)]
        + [pl.BlockSpec(memory_space=pltpu.VMEM)] * 4,
        scratch_shapes=[pltpu.VMEM((2 * rows, 256), jnp.float32)]
        + [pltpu.VMEM((2 * rows, CHUNK), jnp.bfloat16)] * 2
        + [pltpu.VMEM((256, CHUNK), jnp.bfloat16)] * 2,
        name="scatter",
    )(counts, probes, cells, fractions, ky)


def add_cols_kernel(core_ref, low_ref, high_ref, out_ref, first_ref, last_ref):
    row = lax.broadcasted_iota(jnp.int32, (16, 256), 0)
    lane = lax.broadcasted_iota(jnp.int32, (16, 256), 1)
    high_row = row - 8
    put = (row < DAYS) & (lane == COLS * row + (COLS - 1))
    put = put | ((high_row >= 0) & (lane == COLS * (high_row // 2) + high_row % 2))
    width = core_ref.shape[0]
    received = jnp.concatenate([low_ref[:, 0:width], high_ref[:, 0:width]], axis=0)
    out_ref[...] = core_ref[...] + lax.dot_general(
        received,
        jnp.where(put, 1.0, 0.0),
        (((0,), (0,)), ((), ())),
        precision=HIGH,
        preferred_element_type=jnp.float32,
    )
    first, last = [], []
    for q in range(PROBES):
        first.append(out_ref[q * XP : q * XP + 1, :])
        last.append(out_ref[q * XP + ROWS + 1 : q * XP + ROWS + 3, :])
    first_ref[...] = jnp.concatenate(first, axis=0)
    last_ref[...] = jnp.concatenate(last, axis=0)


def add_cols(core, low, high):
    return pl.pallas_call(
        add_cols_kernel,
        out_shape=(
            pltpu.VMEM(core.shape, jnp.float32),
            pltpu.VMEM((PROBES, 256), jnp.float32),
            pltpu.VMEM((2 * PROBES, 256), jnp.float32),
        ),
        name="add_cols",
    )(*near(core, low, high))


def add_rows_kernel(core_ref, first_ref, last_ref, out_ref):
    row = lax.broadcasted_iota(jnp.int32, (ROWS, 256), 0)
    for q in range(PROBES):
        tile = core_ref[q * XP + 1 : q * XP + 1 + ROWS, :]
        extra = jnp.where(row == ROWS - 1, first_ref[q : q + 1, :], 0.0)
        extra = jnp.where(row == 0, last_ref[2 * q : 2 * q + 1, :], extra)
        extra = jnp.where(row == 1, last_ref[2 * q + 1 : 2 * q + 2, :], extra)
        tile = (tile + extra).astype(jnp.bfloat16)
        for copy in range(4):
            out_ref[copy * PROBES + q] = tile


def add_rows(core, first, last):
    return pl.pallas_call(
        add_rows_kernel,
        out_shape=pltpu.VMEM((4 * PROBES, ROWS, 256), jnp.bfloat16),
        name="add_rows",
    )(*near(core, first, last))


def mix_x_kernel(grid_ref, kernel_ref, before_ref, after_ref, out_ref, rows_ref):
    blank = jnp.zeros((5, 1024), jnp.float32)
    outer = [after_ref[...].astype(jnp.float32), blank, before_ref[...].astype(jnp.float32)]
    outer = jnp.concatenate(outer, axis=0).astype(jnp.bfloat16)
    outer = jnp.dot(outer, grid_ref[...], preferred_element_type=jnp.float32)
    inner = jnp.dot(kernel_ref[...], grid_ref[...], preferred_element_type=jnp.float32)
    for side in range(2):
        here = slice(128 * side, 128 * side + 128)
        rows_ref[side, 0:8, :] = outer[:, here]
        rows_ref[side, 264:272, :] = outer[:, here]
        rows_ref[side, 8:264, :] = inner[:, here]
    for part in range(4):
        rows = []
        for r in range(STEP):
            start = 7 + PART * part + r
            wide = [rows_ref[side, pl.ds(start, 8, stride=ROWS), :] for side in range(2)]
            rows.append(jnp.concatenate(wide, axis=1))
        rows = jnp.concatenate(rows, axis=0).astype(jnp.bfloat16)
        for copy in range(4):
            out_ref[4 * copy + part] = rows


def mix_x(grid, kernel, before, after):
    return pl.pallas_call(
        mix_x_kernel,
        out_shape=pltpu.VMEM((16, 8 * STEP, 256), jnp.bfloat16),
        scratch_shapes=[pltpu.VMEM((2, 272, 128), jnp.float32)],
        name="mix_x",
    )(*near(grid, kernel, before, after))


def mix_y_kernel(
    place_ref, kt_ref, mixed_ref, k0_ref, k1_ref, k2_ref, k3_ref, out_ref, smooth_ref
):
    rows = 8 * STEP
    low = lax.broadcasted_iota(jnp.int32, (rows, 128), 1) < COLS
    left = [[] for _ in range(DAYS)]
    for pair in range(8):
        even = mixed_ref[2 * pair].astype(jnp.float32)
        odd = mixed_ref[2 * pair + 1].astype(jnp.float32)
        for side in range(2):
            here = slice(128 * side, 128 * side + 128)
            e, o = even[:, here], odd[:, here]
            left[2 * side].append(jnp.where(low, e, pltpu.roll(o, COLS, 1)))
            left[2 * side + 1].append(jnp.where(low, pltpu.roll(e, COLS, 1), o))
    left = jnp.concatenate([jnp.concatenate(part, axis=1) for part in left], axis=0)
    left = left.astype(jnp.bfloat16)
    gap = jnp.zeros((128 - YP, 1024), jnp.bfloat16)
    for half, (one, two) in enumerate(((k0_ref, k1_ref), (k2_ref, k3_ref))):
        kernel = jnp.concatenate([one[...], gap, two[...], gap], axis=0)
        crossed = lax.dot_general(
            left, kernel, (((1,), (1,)), ((), ())), preferred_element_type=jnp.float32
        )
        by_day = [crossed[t * rows : (t + 1) * rows] for t in range(DAYS)]
        for s in range(DAYS):
            total = kt_ref[s, 0] * by_day[0]
            for t in range(1, DAYS):
                total = total + kt_ref[s, t] * by_day[t]
            for which in range(2):
                here = slice(128 * which, 128 * which + 128)
                smooth_ref[which, s * rows : (s + 1) * rows, :] = total[:, here]
        for which in range(2):
            target = (place_ref[0] + 4 - (2 * half + which)) % 4
            for tile in range(8):
                part = smooth_ref[which, pl.ds(tile, DAYS * STEP, stride=8), :]
                out_ref[tile, target] = part.astype(jnp.bfloat16)


def mix_y(place, kt, mixed, pieces):
    return pl.pallas_call(
        mix_y_kernel,
        out_shape=pltpu.VMEM((8, 4, DAYS * STEP, 128), jnp.bfloat16),
        in_specs=[pl.BlockSpec(memory_space=pltpu.SMEM)] * 2
        + [pl.BlockSpec(memory_space=pltpu.VMEM)] * 5,
        scratch_shapes=[pltpu.VMEM((2, DAYS * 8 * STEP, 128), jnp.float32)],
        name="mix_y",
    )(place, kt, *near(mixed, *pieces))


def gather_kernel(
    count_ref,
    smooth_ref,
    cells_ref,
    fractions_ref,
    out_ref,
    wide_ref,
    window_ref,
    sums_ref,
    x0_ref,
    x1_ref,
    y0_ref,
    y1_ref,
    t0_ref,
    t1_ref,
):
    points = out_ref.shape[1]
    rows = STEP * 4 * PROBES
    wide_ref[...] = smooth_ref[...].astype(jnp.float32)
    days = []
    for s in range(DAYS):
        part = [
            wide_ref[pl.ds(s * STEP + r, 4 * PROBES, stride=DAYS * STEP), :] for r in range(STEP)
        ]
        days.append(jnp.concatenate(part, axis=0))
    blank = jnp.zeros((rows, 128), jnp.float32)
    smooth = [jnp.concatenate([day, blank], axis=1) for day in days]
    for late in range(2):
        window = smooth[late] + pltpu.roll(smooth[late + 1], YP, 1)
        window = window + pltpu.roll(smooth[late + 2], 2 * YP, 1)
        window_ref[late * rows : (late + 1) * rows, :] = window.astype(jnp.bfloat16)

    row = lax.broadcasted_iota(jnp.int32, (8 * STEP, CHUNK), 0)
    row = jnp.where(row // 8 < PART, PART * (row % 4) + row // 8, 8 * XP)

    def prepare(number, x_ref, y_ref, t_ref):
        where = pl.ds(pl.multiple_of(number * CHUNK, CHUNK), CHUNK)
        x_part, y_days, early, late = point_factors(cells_ref, fractions_ref, where, row)
        x_ref[...] = x_part
        y_ref[...] = y_days
        t_ref[0:1, :] = early
        t_ref[1:2, :] = late

    def product(number, x_ref, y_ref, t_ref):
        start = pl.multiple_of(number * CHUNK, CHUNK)
        early, late = t_ref[0:1, :], t_ref[1:2, :]
        hidden = jnp.dot(window_ref[...], y_ref[...], preferred_element_type=jnp.float32)
        total = jnp.zeros((4 * PROBES, CHUNK), jnp.float32)
        for r in range(STEP):
            here = slice(r * 4 * PROBES, (r + 1) * 4 * PROBES)
            timed = early * hidden[here] + late * hidden[rows + here.start : rows + here.stop]
            factor = x_ref[8 * r : 8 * r + 8, :]
            total += timed * jnp.concatenate([factor] * 4, axis=0)
        result = jnp.zeros((PROBES, CHUNK), jnp.float32)
        for side in range(CHUNK // 128):
            sums_ref[side] = total[:, 128 * side : 128 * side + 128]
        for part in range(4):
            piece = [
                sums_ref[side, pl.ds(part, PROBES, stride=4), :] for side in range(CHUNK // 128)
            ]
            result += jnp.concatenate(piece, axis=1)
        result = jnp.where(live_lanes(count_ref, start, CHUNK), result, 0.0)
        out_ref[:, pl.ds(start, CHUNK)] = result.astype(jnp.bfloat16)

    def step(number, carry):
        prepare(2 * number + 1, x1_ref, y1_ref, t1_ref)
        product(2 * number, x0_ref, y0_ref, t0_ref)
        prepare(jnp.minimum(2 * number + 2, points // CHUNK - 1), x0_ref, y0_ref, t0_ref)
        product(2 * number + 1, x1_ref, y1_ref, t1_ref)
        return carry

    prepare(0, x0_ref, y0_ref, t0_ref)
    lax.fori_loop(0, points // CHUNK // 2, step, 0)


def gather(counts, smooth, cells, fractions):
    rows = STEP * 4 * PROBES
    return pl.pallas_call(
        gather_kernel,
        out_shape=jax.ShapeDtypeStruct((PROBES, cells.shape[1]), jnp.bfloat16),
        in_specs=[pl.BlockSpec(memory_space=pltpu.SMEM)]
        + [pl.BlockSpec(memory_space=pltpu.VMEM)] * 3,
        scratch_shapes=[
            pltpu.VMEM((DAYS * rows, 128), jnp.float32),
            pltpu.VMEM((2 * rows, 256), jnp.bfloat16),
            pltpu.VMEM((CHUNK // 128, 4 * PROBES, 128), jnp.float32),
        ]
        + [pltpu.VMEM((8 * STEP, CHUNK), jnp.float32)] * 2
        + [pltpu.VMEM((256, CHUNK), jnp.bfloat16)] * 2
        + [pltpu.VMEM((8, CHUNK), jnp.float32)] * 2,
        name="gather",
    )(counts, *near(smooth, cells, fractions))


def copies_kernel(kernel_ref, out_ref):
    for copy in range(8):
        out_ref[copy] = kernel_ref[...]


def copies(kernel):
    return pl.pallas_call(
        copies_kernel,
        out_shape=pltpu.VMEM((8,) + kernel.shape, kernel.dtype),
        name="copies",
    )(kernel)


def up(count):
    return [(i, i + 1) for i in range(count - 1)]


def down(count):
    return [(i + 1, i) for i in range(count - 1)]


def turns(piece, axis):
    return [piece] + [
        lax.ppermute(piece, axis, [(i, (i + shift) % 4) for i in range(4)]) for shift in (1, 2, 3)
    ]


def body(probes, cells, fractions, counts, kx, ky, kt):
    kernel = lax.all_to_all(copies(kx), NEAR, 0, 0, tiled=True).reshape(8 * ROWS, 1024)
    core, low, high = scatter(counts, probes, cells, fractions, ky)
    low = lax.ppermute(low, GY, down(16))
    high = lax.ppermute(high, GY, up(16))
    core, first, last = add_cols(core, low, high)
    first, last, kernel = lax.optimization_barrier((first, last, kernel))
    first = lax.ppermute(first, GX, down(32))
    last = lax.ppermute(last, GX, up(32))
    grid = add_rows(core, first, last)
    grid, ky, kernel = lax.optimization_barrier((grid, ky, kernel))
    grid = lax.all_to_all(grid, GX, 0, 0, tiled=True)
    before = lax.ppermute(kernel[8 * ROWS - 1 :], "zh", up(4))
    after = lax.ppermute(kernel[0:2], "zh", down(4))
    right = low[:, RIM:].reshape(2, 1024).astype(ky.dtype)
    left = high[0:4, RIM:].reshape(1, 1024).astype(ky.dtype)
    blank = jnp.zeros((YP - COLS - 3, 1024), ky.dtype)
    ky_pieces = turns(jnp.concatenate([left, ky, right, blank], axis=0), "y")
    place = lax.axis_index("y").astype(jnp.int32).reshape(1)
    rest = (grid, ky_pieces, place, before, after)
    grid, ky_pieces, place, before, after = lax.optimization_barrier(rest)
    mixed = mix_x(grid.reshape(32 * ROWS, 256), kernel, before, after)
    mixed = lax.all_to_all(mixed, GY, 0, 0, tiled=True)
    smooth = mix_y(place, kt, mixed, ky_pieces).reshape(32, DAYS * STEP, 128)
    smooth = lax.all_to_all(smooth, HOME, 0, 0, tiled=True)
    return gather(counts, smooth.reshape(32 * DAYS * STEP, 128), cells, fractions)


def solution(mesh):
    fine = Mesh(mesh.devices.reshape(4, 4, 2, 4, 4), AXES)
    return jax.shard_map(
        body,
        mesh=fine,
        in_specs=(
            P(None, AXES),
            P(None, AXES),
            P(None, AXES),
            P(GX, GY),
            P(GX, None),
            P(GY, None),
            P(),
        ),
        out_specs=P(None, AXES),
        check_vma=False,
    )
```

```python
import jax
import jax.numpy as jnp
from jax import lax
from jax.experimental import pallas as pl
from jax.experimental.pallas import tpu as pltpu
from jax.sharding import Mesh
from jax.sharding import PartitionSpec as P

DAYS = 4
PROBES = 8
BLOCK = 128
ROWS = 32
COLS = 64
XP = 40
PART = 9
STEP = PART
BLOCK_ROWS = 40
YP = 80
YD = 72
RIM = 384
CHUNK = 1024
AXES = ("zh", "zl", "c", "x", "y")
GX = ("zh", "zl", "c")
NEAR = ("zl", "c")
HOME = ("zl", "c", "y")
GY = ("x", "y")
HIGH = lax.Precision.HIGHEST


def near(*arrays):
    return [pltpu.with_memory_space_constraint(array, pltpu.VMEM) for array in arrays]


def keys_weights(fraction):
    first = ((-0.5 * fraction + 1.0) * fraction - 0.5) * fraction
    second = (1.5 * fraction - 2.5) * fraction * fraction + 1.0
    third = ((-1.5 * fraction + 2.0) * fraction + 0.5) * fraction
    fourth = (0.5 * fraction - 0.5) * fraction * fraction
    return (first, second, third, fourth)


def spread(cell, weights, row):
    row = row - cell
    result = jnp.where(row == 3, weights[3], 0.0)
    for k in (2, 1, 0):
        result = jnp.where(row == k, weights[k], result)
    return result


def point_factors(cells_ref, fractions_ref, where, row):
    col = lax.broadcasted_iota(jnp.int32, (YD, CHUNK), 0)
    weights = keys_weights(fractions_ref[0:2, where])
    x_part = spread(cells_ref[0:1, where] & (ROWS - 1), [w[0:1] for w in weights], row)
    y_part = spread(cells_ref[1:2, where] & (COLS - 1), [w[1:2] for w in weights], col)
    day = cells_ref[2:3, where]
    y_days = [jnp.where(day == d, y_part, 0.0) for d in range(DAYS - 1)]
    y_days.append(jnp.zeros((256 - 3 * YD, CHUNK), jnp.float32))
    y_days = jnp.concatenate(y_days, axis=0).astype(jnp.bfloat16)
    late = fractions_ref[2:3, where]
    return x_part, y_days, 1.0 - late, late


def live_lanes(count_ref, start, size):
    slot = start + lax.broadcasted_iota(jnp.int32, (1, size), 1)
    return slot // BLOCK < count_ref[0, 0]


def scatter_kernel(
    count_ref,
    probes_ref,
    cells_ref,
    fractions_ref,
    ky_ref,
    core_ref,
    low_ref,
    high_ref,
    acc_ref,
    left0_ref,
    left1_ref,
    right0_ref,
    right1_ref,
):
    chunks = probes_ref.shape[1] // CHUNK
    acc_ref[...] = jnp.zeros_like(acc_ref)

    def prepare(number, left_ref, right_ref):
        start = pl.multiple_of(number * CHUNK, CHUNK)
        where = pl.ds(start, CHUNK)
        row = lax.broadcasted_iota(jnp.int32, (XP, CHUNK), 0)
        x_part, y_days, early, late = point_factors(cells_ref, fractions_ref, where, row)
        values = jnp.where(
            live_lanes(count_ref, start, CHUNK), probes_ref[:, where].astype(jnp.float32), 0.0
        )
        parts = []
        for weight in (early, late):
            timed = weight * values
            for q in range(PROBES):
                parts.append(timed[q : q + 1] * x_part)
        left_ref[...] = jnp.concatenate(parts, axis=0).astype(jnp.bfloat16)
        right_ref[...] = y_days

    def product(left_ref, right_ref):
        acc_ref[...] += lax.dot_general(
            left_ref[...],
            right_ref[...],
            (((1,), (1,)), ((), ())),
            preferred_element_type=jnp.float32,
        )

    def step(number, carry):
        product(left0_ref, right0_ref)
        prepare(2 * number + 1, left1_ref, right1_ref)
        product(left1_ref, right1_ref)
        prepare(jnp.minimum(2 * number + 2, chunks - 1), left0_ref, right0_ref)
        return carry

    prepare(0, left0_ref, right0_ref)
    lax.fori_loop(0, chunks // 2, step, 0)
    rows = PROBES * XP
    blank = jnp.zeros((rows, 128), jnp.float32)
    first = jnp.concatenate([acc_ref[0:rows, :], blank], axis=1)
    second = jnp.concatenate([acc_ref[rows : 2 * rows, :], blank], axis=1)
    total = first + pltpu.roll(second, YD, 1)
    lane = lax.broadcasted_iota(jnp.int32, (rows, 384), 1)
    core = pltpu.roll(total, 383, 1)
    for t in range(1, DAYS):
        core = jnp.where(lane // COLS == t, pltpu.roll(total, 384 - ((YD - COLS) * t + 1), 1), core)
    core_ref[...] = core[:, 0:256]
    out_row = lax.broadcasted_iota(jnp.int32, (16, 384), 0)
    in_lane = lax.broadcasted_iota(jnp.int32, (16, 384), 1)
    low = (out_row < DAYS) & (in_lane == YD * out_row)
    high_row = out_row - 8
    high = (high_row >= 0) & (in_lane == YD * (high_row // 2) + (COLS + 1) + high_row % 2)
    pick = jnp.where(low | high, 1.0, 0.0)
    rims = lax.dot_general(
        pick, total, (((1,), (1,)), ((), ())), precision=HIGH, preferred_element_type=jnp.float32
    )
    top = ky_ref[0:16, :].astype(jnp.float32)
    end = ky_ref[COLS - 16 : COLS, :].astype(jnp.float32)
    low_ref[:, 0:rows] = rims[0:8]
    high_ref[:, 0:rows] = rims[8:16]
    for n in range(4):
        here = slice(256 * n, 256 * n + 256)
        for r in range(2):
            low_ref[4 * r + n : 4 * r + n + 1, RIM:] = top[r : r + 1, here]
        high_ref[n : n + 1, RIM:] = end[15:16, here]
    high_ref[4:8, RIM:] = jnp.zeros((4, 256), jnp.float32)
    low_ref[:, rows:RIM] = jnp.zeros((8, RIM - rows), jnp.float32)
    high_ref[:, rows:RIM] = jnp.zeros((8, RIM - rows), jnp.float32)


def scatter(counts, probes, cells, fractions, ky):
    rows = PROBES * XP
    return pl.pallas_call(
        scatter_kernel,
        out_shape=(
            pltpu.VMEM((rows, 256), jnp.float32),
            pltpu.VMEM((8, RIM + 256), jnp.float32),
            pltpu.VMEM((8, RIM + 256), jnp.float32),
        ),
        in_specs=[pl.BlockSpec(memory_space=pltpu.SMEM)]
        + [pl.BlockSpec(memory_space=pltpu.VMEM)] * 4,
        scratch_shapes=[pltpu.VMEM((2 * rows, 256), jnp.float32)]
        + [pltpu.VMEM((2 * rows, CHUNK), jnp.bfloat16)] * 2
        + [pltpu.VMEM((256, CHUNK), jnp.bfloat16)] * 2,
        name="scatter",
    )(counts, probes, cells, fractions, ky)


def add_cols_kernel(core_ref, low_ref, high_ref, out_ref, first_ref, last_ref):
    row = lax.broadcasted_iota(jnp.int32, (16, 256), 0)
    lane = lax.broadcasted_iota(jnp.int32, (16, 256), 1)
    high_row = row - 8
    put = (row < DAYS) & (lane == COLS * row + (COLS - 1))
    put = put | ((high_row >= 0) & (lane == COLS * (high_row // 2) + high_row % 2))
    width = core_ref.shape[0]
    received = jnp.concatenate([low_ref[:, 0:width], high_ref[:, 0:width]], axis=0)
    out_ref[...] = core_ref[...] + lax.dot_general(
        received,
        jnp.where(put, 1.0, 0.0),
        (((0,), (0,)), ((), ())),
        precision=HIGH,
        preferred_element_type=jnp.float32,
    )
    first, last = [], []
    for q in range(PROBES):
        first.append(out_ref[q * XP : q * XP + 1, :])
        last.append(out_ref[q * XP + ROWS + 1 : q * XP + ROWS + 3, :])
    first_ref[...] = jnp.concatenate(first, axis=0)
    last_ref[...] = jnp.concatenate(last, axis=0)


def add_cols(core, low, high):
    return pl.pallas_call(
        add_cols_kernel,
        out_shape=(
            pltpu.VMEM(core.shape, jnp.float32),
            pltpu.VMEM((PROBES, 256), jnp.float32),
            pltpu.VMEM((2 * PROBES, 256), jnp.float32),
        ),
        name="add_cols",
    )(*near(core, low, high))


def add_rows_kernel(core_ref, first_ref, last_ref, out_ref):
    row = lax.broadcasted_iota(jnp.int32, (ROWS, 256), 0)
    for q in range(PROBES):
        tile = core_ref[q * XP + 1 : q * XP + 1 + ROWS, :]
        extra = jnp.where(row == ROWS - 1, first_ref[q : q + 1, :], 0.0)
        extra = jnp.where(row == 0, last_ref[2 * q : 2 * q + 1, :], extra)
        extra = jnp.where(row == 1, last_ref[2 * q + 1 : 2 * q + 2, :], extra)
        tile = (tile + extra).astype(jnp.bfloat16)
        for copy in range(4):
            out_ref[copy * PROBES + q] = tile


def add_rows(core, first, last):
    return pl.pallas_call(
        add_rows_kernel,
        out_shape=pltpu.VMEM((4 * PROBES, ROWS, 256), jnp.bfloat16),
        name="add_rows",
    )(*near(core, first, last))


def mix_x_kernel(grid_ref, kernel_ref, before_ref, after_ref, out_ref, rows_ref):
    blank = jnp.zeros((5, 1024), jnp.float32)
    outer = [after_ref[...].astype(jnp.float32), blank, before_ref[...].astype(jnp.float32)]
    outer = jnp.concatenate(outer, axis=0).astype(jnp.bfloat16)
    outer = jnp.dot(outer, grid_ref[...], preferred_element_type=jnp.float32)
    inner = jnp.dot(kernel_ref[...], grid_ref[...], preferred_element_type=jnp.float32)
    for side in range(2):
        here = slice(128 * side, 128 * side + 128)
        rows_ref[side, 0:8, :] = outer[:, here]
        rows_ref[side, 264:272, :] = outer[:, here]
        rows_ref[side, 8:264, :] = inner[:, here]
    for part in range(4):
        rows = []
        for r in range(STEP):
            start = 7 + PART * part + r
            wide = [rows_ref[side, pl.ds(start, 8, stride=ROWS), :] for side in range(2)]
            rows.append(jnp.concatenate(wide, axis=1))
        rows = jnp.concatenate(rows, axis=0).astype(jnp.bfloat16)
        for copy in range(4):
            out_ref[4 * copy + part] = rows


def mix_x(grid, kernel, before, after):
    return pl.pallas_call(
        mix_x_kernel,
        out_shape=pltpu.VMEM((16, 8 * STEP, 256), jnp.bfloat16),
        scratch_shapes=[pltpu.VMEM((2, 272, 128), jnp.float32)],
        name="mix_x",
    )(*near(grid, kernel, before, after))


def mix_y_kernel(
    place_ref, kt_ref, mixed_ref, k0_ref, k1_ref, k2_ref, k3_ref, out_ref, smooth_ref
):
    rows = 8 * STEP
    low = lax.broadcasted_iota(jnp.int32, (rows, 128), 1) < COLS
    left = [[] for _ in range(DAYS)]
    for pair in range(8):
        even = mixed_ref[2 * pair].astype(jnp.float32)
        odd = mixed_ref[2 * pair + 1].astype(jnp.float32)
        for side in range(2):
            here = slice(128 * side, 128 * side + 128)
            e, o = even[:, here], odd[:, here]
            left[2 * side].append(jnp.where(low, e, pltpu.roll(o, COLS, 1)))
            left[2 * side + 1].append(jnp.where(low, pltpu.roll(e, COLS, 1), o))
    left = jnp.concatenate([jnp.concatenate(part, axis=1) for part in left], axis=0)
    left = left.astype(jnp.bfloat16)
    gap = jnp.zeros((128 - YP, 1024), jnp.bfloat16)
    for half, (one, two) in enumerate(((k0_ref, k1_ref), (k2_ref, k3_ref))):
        kernel = jnp.concatenate([one[...], gap, two[...], gap], axis=0)
        crossed = lax.dot_general(
            left, kernel, (((1,), (1,)), ((), ())), preferred_element_type=jnp.float32
        )
        by_day = [crossed[t * rows : (t + 1) * rows] for t in range(DAYS)]
        for s in range(DAYS):
            total = kt_ref[s, 0] * by_day[0]
            for t in range(1, DAYS):
                total = total + kt_ref[s, t] * by_day[t]
            for which in range(2):
                here = slice(128 * which, 128 * which + 128)
                smooth_ref[which, s * rows : (s + 1) * rows, :] = total[:, here]
        for which in range(2):
            target = (place_ref[0] + 4 - (2 * half + which)) % 4
            for tile in range(8):
                part = smooth_ref[which, pl.ds(tile, DAYS * STEP, stride=8), :]
                out_ref[tile, target] = part.astype(jnp.bfloat16)


def mix_y(place, kt, mixed, pieces):
    return pl.pallas_call(
        mix_y_kernel,
        out_shape=pltpu.VMEM((8, 4, DAYS * STEP, 128), jnp.bfloat16),
        in_specs=[pl.BlockSpec(memory_space=pltpu.SMEM)] * 2
        + [pl.BlockSpec(memory_space=pltpu.VMEM)] * 5,
        scratch_shapes=[pltpu.VMEM((2, DAYS * 8 * STEP, 128), jnp.float32)],
        name="mix_y",
    )(place, kt, *near(mixed, *pieces))


def gather_kernel(
    count_ref,
    smooth_ref,
    cells_ref,
    fractions_ref,
    out_ref,
    wide_ref,
    window_ref,
    sums_ref,
    x0_ref,
    x1_ref,
    y0_ref,
    y1_ref,
    t0_ref,
    t1_ref,
):
    points = out_ref.shape[1]
    rows = STEP * 4 * PROBES
    for source in range(4 * PROBES):
        block = smooth_ref[source].astype(jnp.float32)
        wide_ref[BLOCK_ROWS * source : BLOCK_ROWS * source + DAYS * STEP, :] = block
    days = []
    for s in range(DAYS):
        part = [
            wide_ref[pl.ds(s * STEP + r, 4 * PROBES, stride=BLOCK_ROWS), :] for r in range(STEP)
        ]
        days.append(jnp.concatenate(part, axis=0))
    blank = jnp.zeros((rows, 128), jnp.float32)
    smooth = [jnp.concatenate([day, blank], axis=1) for day in days]
    for late in range(2):
        window = smooth[late] + pltpu.roll(smooth[late + 1], YD, 1)
        window = window + pltpu.roll(smooth[late + 2], 2 * YD, 1)
        window_ref[late * rows : (late + 1) * rows, :] = window.astype(jnp.bfloat16)

    row = lax.broadcasted_iota(jnp.int32, (8 * STEP, CHUNK), 0)
    row = PART * (row % 4) + row // 8

    def prepare(number, x_ref, y_ref, t_ref):
        where = pl.ds(pl.multiple_of(number * CHUNK, CHUNK), CHUNK)
        x_part, y_days, early, late = point_factors(cells_ref, fractions_ref, where, row)
        x_ref[...] = x_part
        y_ref[...] = y_days
        t_ref[0:1, :] = early
        t_ref[1:2, :] = late

    def product(number, x_ref, y_ref, t_ref):
        start = pl.multiple_of(number * CHUNK, CHUNK)
        early, late = t_ref[0:1, :], t_ref[1:2, :]
        hidden = jnp.dot(window_ref[...], y_ref[...], preferred_element_type=jnp.float32)
        total = jnp.zeros((4 * PROBES, CHUNK), jnp.float32)
        for r in range(STEP):
            here = slice(r * 4 * PROBES, (r + 1) * 4 * PROBES)
            timed = early * hidden[here] + late * hidden[rows + here.start : rows + here.stop]
            factor = x_ref[8 * r : 8 * r + 8, :]
            total += timed * jnp.concatenate([factor] * 4, axis=0)
        result = jnp.zeros((PROBES, CHUNK), jnp.float32)
        for side in range(CHUNK // 128):
            sums_ref[side] = total[:, 128 * side : 128 * side + 128]
        for part in range(4):
            piece = [
                sums_ref[side, pl.ds(part, PROBES, stride=4), :] for side in range(CHUNK // 128)
            ]
            result += jnp.concatenate(piece, axis=1)
        result = jnp.where(live_lanes(count_ref, start, CHUNK), result, 0.0)
        out_ref[:, pl.ds(start, CHUNK)] = result.astype(jnp.bfloat16)

    def step(number, carry):
        prepare(2 * number + 1, x1_ref, y1_ref, t1_ref)
        product(2 * number, x0_ref, y0_ref, t0_ref)
        prepare(jnp.minimum(2 * number + 2, points // CHUNK - 1), x0_ref, y0_ref, t0_ref)
        product(2 * number + 1, x1_ref, y1_ref, t1_ref)
        return carry

    prepare(0, x0_ref, y0_ref, t0_ref)
    lax.fori_loop(0, points // CHUNK // 2, step, 0)


def gather(counts, smooth, cells, fractions):
    rows = STEP * 4 * PROBES
    return pl.pallas_call(
        gather_kernel,
        out_shape=jax.ShapeDtypeStruct((PROBES, cells.shape[1]), jnp.bfloat16),
        in_specs=[pl.BlockSpec(memory_space=pltpu.SMEM)]
        + [pl.BlockSpec(memory_space=pltpu.VMEM)] * 3,
        scratch_shapes=[
            pltpu.VMEM((4 * PROBES * BLOCK_ROWS, 128), jnp.float32),
            pltpu.VMEM((2 * rows, 256), jnp.bfloat16),
            pltpu.VMEM((CHUNK // 128, 4 * PROBES, 128), jnp.float32),
        ]
        + [pltpu.VMEM((8 * STEP, CHUNK), jnp.float32)] * 2
        + [pltpu.VMEM((256, CHUNK), jnp.bfloat16)] * 2
        + [pltpu.VMEM((8, CHUNK), jnp.float32)] * 2,
        name="gather",
    )(counts, *near(smooth, cells, fractions))


def copies_kernel(kernel_ref, out_ref, sems):
    sent = [pltpu.make_async_copy(kernel_ref, out_ref.at[n], sems.at[n]) for n in range(8)]
    for copy in sent:
        copy.start()
    for copy in sent:
        copy.wait()


def copies(kernel):
    return pl.pallas_call(
        copies_kernel,
        out_shape=jax.ShapeDtypeStruct((8,) + kernel.shape, kernel.dtype),
        out_specs=pl.BlockSpec(memory_space=pl.ANY),
        scratch_shapes=[pltpu.SemaphoreType.DMA((8,))],
        name="copies",
    )(kernel)


def up(count):
    return [(i, i + 1) for i in range(count - 1)]


def down(count):
    return [(i + 1, i) for i in range(count - 1)]


def turns(piece, axis):
    pieces = [piece]
    for shift in (1, 2, 3):
        pieces.append(lax.ppermute(piece, axis, [(i, (i + shift) % 4) for i in range(4)]))
    return pieces


def step(probes, cells, fractions, counts, kx, ky, kt):
    kernel = lax.all_to_all(copies(kx), NEAR, 0, 0, tiled=True).reshape(8 * ROWS, 1024)
    core, low, high = scatter(counts, probes, cells, fractions, ky)
    low = lax.ppermute(low, GY, down(16))
    high = lax.ppermute(high, GY, up(16))
    core, first, last = add_cols(core, low, high)
    first, last, kernel = lax.optimization_barrier((first, last, kernel))
    first = lax.ppermute(first, GX, down(32))
    last = lax.ppermute(last, GX, up(32))
    before = lax.ppermute(kernel[8 * ROWS - 1 :], "zh", up(4))
    after = lax.ppermute(kernel[0:2], "zh", down(4))
    grid = add_rows(core, first, last)
    grid, ky = lax.optimization_barrier((grid, ky))
    grid = lax.all_to_all(grid, GX, 0, 0, tiled=True)
    right = low[:, RIM:].reshape(2, 1024).astype(ky.dtype)
    left = high[0:4, RIM:].reshape(1, 1024).astype(ky.dtype)
    blank = jnp.zeros((YP - COLS - 3, 1024), ky.dtype)
    ky_pieces = turns(jnp.concatenate([left, ky, right, blank], axis=0), "y")
    place = lax.axis_index("y").astype(jnp.int32).reshape(1)
    rest = (grid, ky_pieces, place, before, after)
    grid, ky_pieces, place, before, after = lax.optimization_barrier(rest)
    mixed = mix_x(grid.reshape(32 * ROWS, 256), kernel, before, after)
    mixed = lax.all_to_all(mixed, GY, 0, 0, tiled=True)
    smooth = mix_y(place, kt, mixed, ky_pieces).reshape(32, DAYS * STEP, 128)
    smooth = lax.all_to_all(smooth, HOME, 0, 0, tiled=True)
    return gather(counts, smooth, cells, fractions)


def solution(mesh):
    fine = Mesh(mesh.devices.reshape(4, 4, 2, 4, 4), AXES)
    return jax.shard_map(
        step,
        mesh=fine,
        in_specs=(
            P(None, AXES),
            P(None, AXES),
            P(None, AXES),
            P(GX, GY),
            P(GX, None),
            P(GY, None),
            P(),
        ),
        out_specs=P(None, AXES),
        check_vma=False,
    )
```
